32 devices in a mesh: groups: 2 (over x), sect: 2 (over core), tile: 8 (over z, y).
Axes of the slice: x: 2, y: 2, z: 4, core: 2. Of those that a mesh axis runs over, the one named last changes fastest.
Arguments:
- features: bfloat16 [4, 16, 64, 512], P(('groups', 'sect'), 'tile'), parts along dimension 0, may hold values from -6 to 6
- conv_first: bfloat16 [3, 3, 3, 512, 512], replicated, may hold values from -0.0546875 to 0.0546875
- bias_first: bfloat16 [512], replicated, may hold values from -3 to 3
- conv_second: bfloat16 [3, 3, 3, 512, 256], replicated, may hold values from -0.0546875 to 0.0546875
- bias_second: bfloat16 [256], replicated, may hold values from -3 to 3
- conv_third: bfloat16 [3, 3, 3, 256, 128], replicated, may hold values from -0.078125 to 0.078125
- bias_third: bfloat16 [128], replicated, may hold values from -3 to 3
Outputs:
- decoded: bfloat16 [4, 64, 256, 128], P(('groups', 'sect'), 'tile'), parts along dimension 0
The draws below stay inside these ranges and needn't reach their ends.
There are 2 independent parts, one for each index of `groups`. The reference program is written for one: setup_inputs(seed, part) draws one part's arguments, and reference() takes and returns one part's arrays. A program takes and returns all parts, laid end to end along the dimension named above; an argument that names none is the same for every part. Nothing has to cross between parts.
All inputs are finite; a program needn't handle non-finite values.
Results may differ from the reference program's by a relative error of at most 0.014.
Values may be sent and summed in bfloat16 or wider, within the bound.
No kernel may reach another device: no remote copies, remote signals or barrier semaphores. Data moves between devices by JAX's collectives and lax.ppermute only.
A program may use at most 128 MiB of HBM per device.

```python
import jax
import jax.numpy as jnp

C1 = 512
C2 = 256
C3 = 128
WA = 64
FRAMES = 2
HA = 16


def block_scale(rng, extent, shards, smallest, high):
    def one(axis_at, shards_of):
        draws = jax.random.uniform(jax.random.fold_in(jax.random.fold_in(rng, 6), axis_at), (shards_of,), jnp.float32, smallest / len(shards), high / len(shards))
        return jnp.repeat(jnp.exp(draws), extent[axis_at] // shards_of).reshape((-1,) + (1,) * (len(extent) - axis_at - 1))

    gain = one(*shards[0])
    for cut in shards[1:]:
        gain = gain * one(*cut)
    return gain


def bell_draw(rng, shape, width, reach, shards=(), dtype=jnp.bfloat16):
    level = block_scale(rng, shape, shards, -0.22, 0.18) if shards else 1.0
    result = jax.random.normal(rng, shape, jnp.float32) * width * level
    return jnp.minimum(jnp.maximum(result, -reach), reach).astype(dtype)


def setup_inputs(seed: int = 0, part: int = 0) -> dict:
    streams_of = jax.random.split(jax.random.key(seed), 8)
    own_keys = jax.random.split(jax.random.fold_in(streams_of[7], part), 8)
    return {
        "features": bell_draw(own_keys[0], (FRAMES, HA, WA, C1), 1.0, 6.0, ((0, 2), (1, 8))),
        "conv_first": bell_draw(streams_of[1], (3, 3, 3, C1, C1), (27 * C1) ** -0.5, 0.0546875),
        "bias_first": bell_draw(streams_of[2], (C1,), 0.5, 3.0),
        "conv_second": bell_draw(streams_of[3], (3, 3, 3, C1, C2), (27 * C1) ** -0.5, 0.0546875),
        "bias_second": bell_draw(streams_of[4], (C2,), 0.5, 3.0),
        "conv_third": bell_draw(streams_of[5], (3, 3, 3, C2, C3), (27 * C2) ** -0.5, 0.078125),
        "bias_third": bell_draw(streams_of[6], (C3,), 0.5, 3.0),
    }


def widen(padded, upsample):
    if upsample:
        padded = jnp.repeat(jnp.repeat(padded, 2, axis=0), 2, axis=1)[1:-1]
    return jnp.pad(padded, ((0, 0), (1, 1), (0, 0)))


def apply_taps(cur_pad, prev_pad, weight, offset):
    row_count = cur_pad.shape[0] - 2
    col_count = cur_pad.shape[1] - 2
    chan_count = cur_pad.shape[2]
    summed = jnp.zeros((row_count * col_count, weight.shape[4]), jnp.float32)
    for row_tap in range(3):
        for col_tap in range(3):
            cur_win = cur_pad[row_tap:row_tap + row_count, col_tap:col_tap + col_count].reshape(row_count * col_count, chan_count)
            prev_win = prev_pad[row_tap:row_tap + row_count, col_tap:col_tap + col_count].reshape(row_count * col_count, chan_count)
            summed = summed + (jnp.dot(prev_win, weight[0, row_tap, col_tap], preferred_element_type=jnp.float32)
                               + jnp.dot(prev_win, weight[1, row_tap, col_tap], preferred_element_type=jnp.float32)
                               + jnp.dot(cur_win, weight[2, row_tap, col_tap], preferred_element_type=jnp.float32))
    return summed.reshape(row_count, col_count, -1) + offset.astype(jnp.float32)


def causal(active, weight, offset, upsample):
    earlier = widen(jnp.pad(active[0], ((1, 1), (0, 0), (0, 0))), upsample)
    later = widen(jnp.pad(active[1], ((1, 1), (0, 0), (0, 0))), upsample)
    return jnp.stack([apply_taps(earlier, earlier, weight, offset), apply_taps(later, earlier, weight, offset)])


def reference(features, conv_first, bias_first, conv_second, bias_second, conv_third, bias_third):
    silu_in = jax.nn.silu(features.astype(jnp.float32)).astype(jnp.bfloat16)
    hidden = (features.astype(jnp.float32) + causal(silu_in, conv_first, bias_first, False)).astype(jnp.bfloat16)
    silu_mid = jax.nn.silu(hidden.astype(jnp.float32)).astype(jnp.bfloat16)
    silu_low = jax.nn.silu(causal(silu_mid, conv_second, bias_second, True)).astype(jnp.bfloat16)
    return causal(silu_low, conv_third, bias_third, True).astype(jnp.bfloat16)
```

```python
import functools

import jax
import jax.numpy as jnp
from jax import lax
from jax.experimental import pallas as pl
from jax.experimental.pallas import tpu as pltpu
from jax.sharding import PartitionSpec as P

F32 = jnp.float32
BF16 = jnp.bfloat16


def silu(v):
    return v / (1.0 + jnp.exp(-v))


def shifted(v):
    count = v.shape[0]
    column = lax.broadcasted_iota(jnp.int32, v.shape, 0)
    before = jnp.where(column == 0, 0.0, pltpu.roll(v, 1, 0))
    after = jnp.where(column == count - 1, 0.0, pltpu.roll(v, count - 1, 0))
    return before, after


def dot(a, b):
    return jnp.dot(a, b, preferred_element_type=F32)


def merge_time(source, target):
    cin = source.shape[3]
    step = 32

    def body(n, _):
        at = pl.multiple_of(n * step, step)
        for i in range(3):
            for j in range(3):
                total = source[0, i, j, pl.ds(at, step), :] + source[1, i, j, pl.ds(at, step), :]
                target[i, pl.ds(j * cin + at, step), :] = total
        return 0

    lax.fori_loop(0, cin // step, body, 0)


def merge_space(source, target, step):
    cin, cout = source.shape[3], source.shape[4]

    def body(n, _):
        at = pl.multiple_of(n * step, step)
        for t in range(2):
            tap = {}
            for i in range(3):
                for j in range(3):
                    if t == 0:
                        tap[i, j] = source[0, i, j, pl.ds(at, step), :].astype(F32) + source[
                            1, i, j, pl.ds(at, step), :
                        ].astype(F32)
                    else:
                        tap[i, j] = source[2, i, j, pl.ds(at, step), :].astype(F32)
            for a in range(2):
                for i in range(2):
                    if a == i:
                        lo = i
                        row = [tap[lo, j] + tap[lo + 1, j] for j in range(3)]
                    else:
                        row = [tap[2 * i, j] for j in range(3)]
                    for b in range(2):
                        if b == 0:
                            columns = (row[0] + row[1], row[2])
                        else:
                            columns = (row[0], row[1] + row[2])
                        for j in range(2):
                            target[t, b, i, pl.ds(j * cin + at, step), pl.ds(a * cout, cout)] = columns[
                                j
                            ].astype(BF16)
        return 0

    lax.fori_loop(0, cin // step, body, 0)


def kernel(
    flags, own, halo, own0, halo0, w1, b1, w2, b2, w3, b3, out, v1, v2, v3, xcat, mcat, lcat, wide
):
    rows, cols, c1 = own.shape
    c2 = b2.shape[1]
    c3 = b3.shape[1]
    second = flags[0] > 0
    first_tile = flags[1] > 0
    last_tile = flags[2] > 0
    merge_time(w1, v1)
    merge_space(w2, v2, 16)
    merge_space(w3, v3, 16)

    def feature(f, r):
        if r < 2:
            mine, other = halo[r], halo0[r]
        elif r < rows + 2:
            mine, other = own[r - 2], own0[r - 2]
        else:
            mine, other = halo[r - rows], halo0[r - rows]
        mine = mine.astype(F32)
        if f == 1:
            return mine
        return jnp.where(second, other.astype(F32), mine)

    for f in range(2):
        for r in range(rows + 4):
            v = silu(feature(f, r))
            before, after = shifted(v)
            xcat[f, r, :, 0:c1] = before.astype(BF16)
            xcat[f, r, :, c1 : 2 * c1] = v.astype(BF16)
            xcat[f, r, :, 2 * c1 : 3 * c1] = after.astype(BF16)

    mrows = rows + 2
    early = jnp.zeros((mrows * cols, c1), F32)
    now = [early, early]
    for i in range(3):
        lhs = [xcat[f, i : i + mrows].reshape(mrows * cols, 3 * c1) for f in range(2)]
        early = early + dot(lhs[0], v1[i])
        for f in range(2):
            now[f] = now[f] + dot(lhs[f], w1[2, i].reshape(3 * c1, c1))
    bias = b1[...].astype(F32)
    for f in range(2):
        total = early + now[f] + bias
        for m in range(mrows):
            v = total[m * cols : (m + 1) * cols] + feature(f, m + 1)
            v = silu(v.astype(BF16).astype(F32))
            if m == 0:
                v = jnp.where(first_tile, 0.0, v)
            if m == mrows - 1:
                v = jnp.where(last_tile, 0.0, v)
            before, after = shifted(v)
            mcat[f, m, :, 0:c1] = before.astype(BF16)
            mcat[f, m, :, c1 : 2 * c1] = v.astype(BF16)
            mcat[f, m, :, 2 * c1 : 3 * c1] = after.astype(BF16)

    wins = mrows - 1
    bias = b2[...].astype(F32)
    for b in range(2):
        lanes = slice(c1, 3 * c1) if b == 0 else slice(0, 2 * c1)
        early = jnp.zeros((wins * cols, 2 * c2), F32)
        now = [early, early]
        for i in range(2):
            lhs = [mcat[f, i : i + wins, :, lanes].reshape(wins * cols, 2 * c1) for f in range(2)]
            early = early + dot(lhs[0], v2[0, b, i])
            for f in range(2):
                now[f] = now[f] + dot(lhs[f], v2[1, b, i])
        for f in range(2):
            total = early + now[f]
            for w in range(wins):
                for a in range(2):
                    v = total[w * cols : (w + 1) * cols, a * c2 : (a + 1) * c2] + bias
                    v = silu(v)
                    if w == 0 and a == 0:
                        v = jnp.where(first_tile, 0.0, v)
                    if w == wins - 1 and a == 1:
                        v = jnp.where(last_tile, 0.0, v)
                    before, after = shifted(v)
                    r = 2 * w + a
                    if b == 0:
                        lcat[f, r, :, 0:c2] = before.astype(BF16)
                        lcat[f, r, :, 2 * c2 : 3 * c2] = v.astype(BF16)
                    else:
                        lcat[f, r, :, c2 : 2 * c2] = v.astype(BF16)
                        lcat[f, r, :, 3 * c2 : 4 * c2] = after.astype(BF16)

    lrows = 2 * wins
    wins = lrows - 1
    bias = b3[...].astype(F32)
    for q in range(4):
        b = 1 if q % 2 == 0 else 0
        at = (0, c2, c2, 2 * c2)[q]
        total = jnp.zeros((wins * cols, 2 * c3), F32)
        for i in range(2):
            for f in range(2):
                lhs = lcat[f, i : i + wins, :, at : at + 2 * c2].reshape(wins * cols, 2 * c2)
                total = total + dot(lhs, v3[f, b, i])
        for o in range(4 * rows):
            a = 1 - o % 2
            w = (o + 1) // 2
            v = total[w * cols : (w + 1) * cols, a * c3 : (a + 1) * c3] + bias
            wide[o, pl.ds(q, cols, stride=4), :] = v
    for o in range(4 * rows):
        out[o] = wide[o].astype(BF16)


def in_vmem(x):
    return pltpu.with_memory_space_constraint(x, pltpu.VMEM)


def per_device(features, conv_first, bias_first, conv_second, bias_second, conv_third, bias_third):
    own = features[0]
    rows, cols, c1 = own.shape
    c2 = conv_second.shape[4]
    c3 = conv_third.shape[4]
    tiles = lax.axis_size("tile")
    forward = [(i, i + 1) for i in range(tiles - 1)]
    backward = [(i + 1, i) for i in range(tiles - 1)]
    across = [(0, 1)]
    own0 = lax.ppermute(own, "sect", across)
    top = lax.ppermute(own[rows - 2 :], "tile", forward)
    bottom = lax.ppermute(own[:2], "tile", backward)
    halo = jnp.concatenate([top, bottom], axis=0)
    halo0 = lax.ppermute(halo, "sect", across)
    tile = lax.axis_index("tile")
    flags = jnp.stack([lax.axis_index("sect"), (tile == 0).astype(jnp.int32), (tile == tiles - 1).astype(jnp.int32)])
    vmem = pl.BlockSpec(memory_space=pltpu.VMEM)
    out = pl.pallas_call(
        kernel,
        out_shape=jax.ShapeDtypeStruct((4 * rows, 4 * cols, c3), BF16),
        in_specs=[pl.BlockSpec(memory_space=pltpu.SMEM)] + [vmem] * 10,
        out_specs=vmem,
        scratch_shapes=[
            pltpu.VMEM((3, 3 * c1, c1), BF16),
            pltpu.VMEM((2, 2, 2, 2 * c1, 2 * c2), BF16),
            pltpu.VMEM((2, 2, 2, 2 * c2, 2 * c3), BF16),
            pltpu.VMEM((2, rows + 4, cols, 3 * c1), BF16),
            pltpu.VMEM((2, rows + 2, cols, 3 * c1), BF16),
            pltpu.VMEM((2, 2 * rows + 2, cols, 4 * c2), BF16),
            pltpu.VMEM((4 * rows, 4 * cols, c3), F32),
        ],
        compiler_params=pltpu.CompilerParams(vmem_limit_bytes=36 << 20),
    )(
        flags,
        own,
        halo,
        own0,
        halo0,
        in_vmem(conv_first),
        bias_first.reshape(1, c1),
        in_vmem(conv_second),
        bias_second.reshape(1, c2),
        in_vmem(conv_third),
        bias_third.reshape(1, c3),
    )
    return out[None]


def solution(mesh):
    return jax.shard_map(
        per_device,
        mesh=mesh,
        in_specs=(P(("groups", "sect"), "tile", None, None), P(), P(), P(), P(), P(), P()),
        out_specs=P(("groups", "sect"), "tile", None, None),
        check_vma=False,
    )
```

```python
import jax
import jax.numpy as jnp
from jax import lax
from jax.experimental import pallas as pl
from jax.experimental.pallas import tpu as pltpu
from jax.sharding import PartitionSpec as P

F32 = jnp.float32
BF16 = jnp.bfloat16


def silu(v):
    return v / (1.0 + jnp.exp(-v))


def shifted(v):
    count = v.shape[0]
    column = lax.broadcasted_iota(jnp.int32, v.shape, 0)
    before = jnp.where(column == 0, 0.0, pltpu.roll(v, 1, 0))
    after = jnp.where(column == count - 1, 0.0, pltpu.roll(v, count - 1, 0))
    return before, after


def dot(a, b):
    return jnp.dot(a, b, preferred_element_type=F32)


def merge_time(source, target):
    cin = source.shape[2]
    step = 64

    def body(n, _):
        at = pl.multiple_of(n * step, step)
        for j in range(3):
            total = source[0, j, pl.ds(at, step), :] + source[1, j, pl.ds(at, step), :]
            target[pl.ds(j * cin + at, step), :] = total
        return 0

    lax.fori_loop(0, cin // step, body, 0)


def merge_space(source, target, step):
    cin, cout = source.shape[3], source.shape[4]

    def body(n, _):
        at = pl.multiple_of(n * step, step)
        for t in range(2):
            tap = {}
            for i in range(3):
                for j in range(3):
                    if t == 0:
                        tap[i, j] = source[0, i, j, pl.ds(at, step), :].astype(F32) + source[
                            1, i, j, pl.ds(at, step), :
                        ].astype(F32)
                    else:
                        tap[i, j] = source[2, i, j, pl.ds(at, step), :].astype(F32)
            for a in range(2):
                for i in range(2):
                    if a == i:
                        lo = i
                        row = [tap[lo, j] + tap[lo + 1, j] for j in range(3)]
                    else:
                        row = [tap[2 * i, j] for j in range(3)]
                    for b in range(2):
                        if b == 0:
                            columns = (row[0] + row[1], row[2])
                        else:
                            columns = (row[0], row[1] + row[2])
                        for j in range(2):
                            target[t, b, i, pl.ds(j * cin + at, step), pl.ds(a * cout, cout)] = columns[
                                j
                            ].astype(BF16)
        return 0

    lax.fori_loop(0, cin // step, body, 0)


def put_cat(target, at, v):
    chans = v.shape[1]
    before, after = shifted(v)
    target[(*at, slice(None), slice(0, chans))] = before.astype(BF16)
    target[(*at, slice(None), slice(chans, 2 * chans))] = v.astype(BF16)
    target[(*at, slice(None), slice(2 * chans, 3 * chans))] = after.astype(BF16)


def early_kernel(pair, w1, acc, v1, wn, cat, raw, sems):
    rows, cols, c1 = pair.shape[1:]
    second = lax.axis_index("sect") > 0

    def copy(t, i):
        target = raw.at[i, t] if t < 2 else wn.at[i]
        return pltpu.make_async_copy(w1.at[t, i], target, sems.at[i, t])

    for i in range(3):
        for t in range(3):
            copy(t, i).start()
    for r in range(rows):
        mine, other = pair[0, r].astype(F32), pair[1, r].astype(F32)
        put_cat(cat, (0, r), silu(jnp.where(second, other, mine)))
        put_cat(cat, (1, r), silu(mine))
    size = rows * cols
    acc[...] = jnp.zeros(acc.shape, F32)

    def tap(i, _):
        for t in range(3):
            copy(t, i).wait()
        merge_time(raw.at[i], v1.at[i])
        both = cat[...].reshape(2 * size, 3 * c1)
        part = dot(both[:size], v1[i])
        total = dot(both, wn[i].reshape(3 * c1, c1))
        for f in range(2):
            value = (total[f * size : (f + 1) * size] + part).reshape(rows, cols, c1)
            acc[f, pl.ds(2 - i, rows)] += value
        return 0

    lax.fori_loop(0, 3, tap, 0)


def late_kernel(
    pair, far, near, acc, v1, wn, b1, w2, b2, w3, b3, out, hcat, mcat, lcat, wide, r2, r3, v2, v3, sems
):
    rows, cols, c1 = pair.shape[1:]
    c2 = b2.shape[0]
    c3 = b3.shape[0]
    second = lax.axis_index("sect") > 0
    tile = lax.axis_index("tile")
    first_tile = tile == 0
    last_tile = tile == lax.axis_size("tile") - 1
    copies = [
        pltpu.make_async_copy(w2, r2, sems.at[0]),
        pltpu.make_async_copy(w3, r3, sems.at[1]),
    ]
    for copy in copies:
        copy.start()

    def feature(f, r):
        if r < 2:
            if f == 0:
                return jnp.where(second, far[0, r].astype(F32), near[0, r].astype(F32))
            return jnp.where(second, far[1, r].astype(F32), near[0, r].astype(F32))
        if r < rows + 2:
            mine = pair[0, r - 2].astype(F32)
            if f == 1:
                return mine
            return jnp.where(second, pair[1, r - 2].astype(F32), mine)
        r = r - rows - 2
        if f == 0:
            return jnp.where(second, near[1, r].astype(F32), far[1, r].astype(F32))
        return jnp.where(second, near[0, r].astype(F32), far[1, r].astype(F32))

    mrows = rows + 2
    for f in range(2):
        for r in range(4):
            put_cat(hcat, (f, r), silu(feature(f, r if r < 2 else r + rows)))
    size = 2 * cols

    def tap(i, _):
        lhs = jnp.concatenate([hcat[f, pl.ds(i, 2)].reshape(size, 3 * c1) for f in range(2)], axis=0)
        part = dot(lhs[:size], v1[i])
        total = dot(lhs, wn[i].reshape(3 * c1, c1))
        for f in range(2):
            value = (total[f * size : (f + 1) * size] + part).reshape(2, cols, c1)
            acc[f, jnp.where(i < 2, 0, rows)] += value[0]
            acc[f, jnp.where(i < 1, 1, rows + 1)] += value[1]
        return 0

    lax.fori_loop(0, 3, tap, 0)
    bias = b1[...].astype(F32)[None, :]
    for f in range(2):
        for m in range(mrows):
            v = acc[f, m] + bias + feature(f, m + 1)
            v = silu(v.astype(BF16).astype(F32))
            if m == 0:
                v = jnp.where(first_tile, 0.0, v)
            if m == mrows - 1:
                v = jnp.where(last_tile, 0.0, v)
            put_cat(mcat, (f, m), v)

    copies[0].wait()
    merge_space(r2, v2, 16)
    copies[1].wait()
    merge_space(r3, v3, 16)

    wins = mrows - 1
    bias = b2[...].astype(F32)[None, :]
    for b in range(2):
        lanes = slice(c1, 3 * c1) if b == 0 else slice(0, 2 * c1)
        early = jnp.zeros((wins * cols, 2 * c2), F32)
        now = [early, early]
        for i in range(2):
            lhs = [mcat[f, i : i + wins, :, lanes].reshape(wins * cols, 2 * c1) for f in range(2)]
            early = early + dot(lhs[0], v2[0, b, i])
            for f in range(2):
                now[f] = now[f] + dot(lhs[f], v2[1, b, i])
        for f in range(2):
            total = early + now[f]
            for w in range(wins):
                for a in range(2):
                    v = total[w * cols : (w + 1) * cols, a * c2 : (a + 1) * c2] + bias
                    v = silu(v)
                    if w == 0 and a == 0:
                        v = jnp.where(first_tile, 0.0, v)
                    if w == wins - 1 and a == 1:
                        v = jnp.where(last_tile, 0.0, v)
                    before, after = shifted(v)
                    r = 2 * w + a
                    if b == 0:
                        lcat[f, r, :, 0:c2] = before.astype(BF16)
                        lcat[f, r, :, 2 * c2 : 3 * c2] = v.astype(BF16)
                    else:
                        lcat[f, r, :, c2 : 2 * c2] = v.astype(BF16)
                        lcat[f, r, :, 3 * c2 : 4 * c2] = after.astype(BF16)

    lrows = 2 * wins
    wins = lrows - 1
    bias = b3[...].astype(F32)[None, :]
    for q in range(4):
        b = 1 if q % 2 == 0 else 0
        at = (0, c2, c2, 2 * c2)[q]
        total = jnp.zeros((wins * cols, 2 * c3), F32)
        for i in range(2):
            for f in range(2):
                lhs = lcat[f, i : i + wins, :, at : at + 2 * c2].reshape(wins * cols, 2 * c2)
                total = total + dot(lhs, v3[f, b, i])
        for o in range(4 * rows):
            a = 1 - o % 2
            w = (o + 1) // 2
            v = total[w * cols : (w + 1) * cols, a * c3 : (a + 1) * c3] + bias
            wide[o, pl.ds(q, cols, stride=4), :] = v
    for o in range(4 * rows):
        out[o] = wide[o].astype(BF16)


def in_vmem(x):
    return pltpu.with_memory_space_constraint(x, pltpu.VMEM)


def per_device(features, conv_first, bias_first, conv_second, bias_second, conv_third, bias_third):
    own = features[0]
    rows, cols, c1 = own.shape
    c2 = conv_second.shape[4]
    c3 = conv_third.shape[4]
    tiles = lax.axis_size("tile")
    swap = [(0, 1), (1, 0)]
    apart = [(i, tiles + i + 1) for i in range(tiles - 1)]
    apart += [(tiles + i + 1, i) for i in range(tiles - 1)]
    vmem = pl.BlockSpec(memory_space=pltpu.VMEM)
    anywhere = pl.BlockSpec(memory_space=pl.ANY)

    pair = jnp.stack([own, lax.ppermute(own, "sect", swap)])
    if rows == 2:
        edge = pair
    else:
        edge = jnp.where(lax.axis_index("sect") == 0, pair[:, rows - 2 :], pair[:, :2])
    far = lax.ppermute(edge, ("sect", "tile"), apart)
    near = lax.ppermute(far, "sect", swap)
    acc, v1, wn = pl.pallas_call(
        early_kernel,
        out_shape=[
            pltpu.VMEM((2, rows + 2, cols, c1), F32),
            pltpu.VMEM((3, 3 * c1, c1), BF16),
            pltpu.VMEM((3, 3, c1, c1), BF16),
        ],
        in_specs=[vmem, anywhere],
        out_specs=[vmem] * 3,
        scratch_shapes=[
            pltpu.VMEM((2, rows, cols, 3 * c1), BF16),
            pltpu.VMEM((3, 2, 3, c1, c1), BF16),
            pltpu.SemaphoreType.DMA((3, 3)),
        ],
        cost_estimate=pl.CostEstimate(flops=6_000_000_000, bytes_accessed=1024, transcendentals=0),
        compiler_params=pltpu.CompilerParams(vmem_limit_bytes=16 << 20),
    )(in_vmem(pair), pltpu.with_memory_space_constraint(conv_first, pltpu.HBM))
    out = pl.pallas_call(
        late_kernel,
        out_shape=jax.ShapeDtypeStruct((4 * rows, 4 * cols, c3), BF16),
        in_specs=[vmem] * 7 + [anywhere, vmem, anywhere, vmem],
        out_specs=vmem,
        scratch_shapes=[
            pltpu.VMEM((2, 4, cols, 3 * c1), BF16),
            pltpu.VMEM((2, rows + 2, cols, 3 * c1), BF16),
            pltpu.VMEM((2, 2 * rows + 2, cols, 4 * c2), BF16),
            pltpu.VMEM((4 * rows, 4 * cols, c3), F32),
            pltpu.VMEM(conv_second.shape, BF16),
            pltpu.VMEM(conv_third.shape, BF16),
            pltpu.VMEM((2, 2, 2, 2 * c1, 2 * c2), BF16),
            pltpu.VMEM((2, 2, 2, 2 * c2, 2 * c3), BF16),
            pltpu.SemaphoreType.DMA((2,)),
        ],
        cost_estimate=pl.CostEstimate(flops=8_000_000_000, bytes_accessed=1024, transcendentals=0),
        compiler_params=pltpu.CompilerParams(vmem_limit_bytes=36 << 20),
    )(
        in_vmem(pair),
        in_vmem(far),
        in_vmem(near),
        in_vmem(acc),
        in_vmem(v1),
        in_vmem(wn),
        bias_first,
        pltpu.with_memory_space_constraint(conv_second, pltpu.HBM),
        bias_second,
        pltpu.with_memory_space_constraint(conv_third, pltpu.HBM),
        bias_third,
    )
    return out[None]


def solution(mesh):
    return jax.shard_map(
        per_device,
        mesh=mesh,
        in_specs=(P(("groups", "sect"), "tile", None, None), P(), P(), P(), P(), P(), P()),
        out_specs=P(("groups", "sect"), "tile", None, None),
        check_vma=False,
    )
```

```python
import jax
import jax.numpy as jnp
from jax import lax
from jax.experimental import pallas as pl
from jax.experimental.pallas import tpu as pltpu
from jax.sharding import PartitionSpec as P

F32 = jnp.float32
BF16 = jnp.bfloat16


def silu(v):
    return v / (1.0 + jnp.exp(-v))


def shifted(v):
    count = v.shape[0]
    column = lax.broadcasted_iota(jnp.int32, v.shape, 0)
    before = jnp.where(column == 0, 0.0, pltpu.roll(v, 1, 0))
    after = jnp.where(column == count - 1, 0.0, pltpu.roll(v, count - 1, 0))
    return before, after


def dot(a, b):
    return jnp.dot(a, b, preferred_element_type=F32)


def merge_time(source, target):
    cin = source.shape[2]
    step = 64

    def body(n, _):
        at = pl.multiple_of(n * step, step)
        for j in range(3):
            total = source[0, j, pl.ds(at, step), :] + source[1, j, pl.ds(at, step), :]
            target[pl.ds(j * cin + at, step), :] = total
        return 0

    lax.fori_loop(0, cin // step, body, 0)


def merge_space(source, target, step):
    cin, cout = source.shape[3], source.shape[4]

    def body(n, _):
        at = pl.multiple_of(n * step, step)
        for t in range(2):
            tap = {}
            for i in range(3):
                for j in range(3):
                    if t == 0:
                        tap[i, j] = source[0, i, j, pl.ds(at, step), :].astype(F32) + source[
                            1, i, j, pl.ds(at, step), :
                        ].astype(F32)
                    else:
                        tap[i, j] = source[2, i, j, pl.ds(at, step), :].astype(F32)
            for a in range(2):
                for i in range(2):
                    if a == i:
                        lo = i
                        row = [tap[lo, j] + tap[lo + 1, j] for j in range(3)]
                    else:
                        row = [tap[2 * i, j] for j in range(3)]
                    for b in range(2):
                        if b == 0:
                            columns = (row[0] + row[1], row[2])
                        else:
                            columns = (row[0], row[1] + row[2])
                        for j in range(2):
                            target[t, b, i, pl.ds(j * cin + at, step), pl.ds(a * cout, cout)] = columns[
                                j
                            ].astype(BF16)
        return 0

    lax.fori_loop(0, cin // step, body, 0)


def put_cat(target, at, v):
    chans = v.shape[1]
    before, after = shifted(v)
    target[(*at, slice(None), slice(0, chans))] = before.astype(BF16)
    target[(*at, slice(None), slice(chans, 2 * chans))] = v.astype(BF16)
    target[(*at, slice(None), slice(2 * chans, 3 * chans))] = after.astype(BF16)


def pair_kernel(own, other, pair):
    pair[0] = own[...]
    pair[1] = other[...]


def early_kernel(pair, w1, w2, w3, acc, v1, wn, v2, v3, cat, raw, sems):
    rows, cols, c1 = pair.shape[1:]
    second = lax.axis_index("sect") > 0

    def copy(t, i):
        target = raw.at[i, t] if t < 2 else wn.at[i]
        return pltpu.make_async_copy(w1.at[t, i], target, sems.at[i, t])

    for i in range(3):
        for t in range(3):
            copy(t, i).start()
    for r in range(rows):
        mine, other = pair[0, r].astype(F32), pair[1, r].astype(F32)
        put_cat(cat, (0, r), silu(jnp.where(second, other, mine)))
        put_cat(cat, (1, r), silu(mine))
    merge_space(w3, v3, 16)
    merge_space(w2, v2, 16)
    size = rows * cols
    acc[...] = jnp.zeros(acc.shape, F32)

    def tap(i, _):
        for t in range(3):
            copy(t, i).wait()
        merge_time(raw.at[i], v1.at[i])
        both = cat[...].reshape(2 * size, 3 * c1)
        part = dot(both[:size], v1[i])
        total = dot(both, wn[i].reshape(3 * c1, c1))
        for f in range(2):
            value = (total[f * size : (f + 1) * size] + part).reshape(rows, cols, c1)
            acc[f, pl.ds(2 - i, rows)] += value
        return 0

    lax.fori_loop(0, 3, tap, 0)


def late_kernel(
    pair, far, near, acc, v1, wn, b1, v2, b2, v3, b3, out, hcat, mcat, lcat, wide
):
    rows, cols, c1 = pair.shape[1:]
    c2 = b2.shape[0]
    c3 = b3.shape[0]
    second = lax.axis_index("sect") > 0
    tile = lax.axis_index("tile")
    first_tile = tile == 0
    last_tile = tile == lax.axis_size("tile") - 1

    def feature(f, r):
        if r < 2:
            if f == 0:
                return jnp.where(second, far[0, r].astype(F32), near[0, r].astype(F32))
            return jnp.where(second, far[1, r].astype(F32), near[0, r].astype(F32))
        if r < rows + 2:
            mine = pair[0, r - 2].astype(F32)
            if f == 1:
                return mine
            return jnp.where(second, pair[1, r - 2].astype(F32), mine)
        r = r - rows - 2
        if f == 0:
            return jnp.where(second, near[1, r].astype(F32), far[1, r].astype(F32))
        return jnp.where(second, near[0, r].astype(F32), far[1, r].astype(F32))

    mrows = rows + 2
    for f in range(2):
        for r in range(4):
            put_cat(hcat, (f, r), silu(feature(f, r if r < 2 else r + rows)))
    size = 2 * cols

    def tap(i, _):
        lhs = jnp.concatenate([hcat[f, pl.ds(i, 2)].reshape(size, 3 * c1) for f in range(2)], axis=0)
        part = dot(lhs[:size], v1[i])
        total = dot(lhs, wn[i].reshape(3 * c1, c1))
        for f in range(2):
            value = (total[f * size : (f + 1) * size] + part).reshape(2, cols, c1)
            acc[f, jnp.where(i < 2, 0, rows)] += value[0]
            acc[f, jnp.where(i < 1, 1, rows + 1)] += value[1]
        return 0

    lax.fori_loop(0, 3, tap, 0)
    bias = b1[...].astype(F32)[None, :]
    for f in range(2):
        for m in range(mrows):
            v = acc[f, m] + bias + feature(f, m + 1)
            v = silu(v.astype(BF16).astype(F32))
            if m == 0:
                v = jnp.where(first_tile, 0.0, v)
            if m == mrows - 1:
                v = jnp.where(last_tile, 0.0, v)
            put_cat(mcat, (f, m), v)

    wins = mrows - 1
    bias = b2[...].astype(F32)[None, :]
    for b in range(2):
        lanes = slice(c1, 3 * c1) if b == 0 else slice(0, 2 * c1)
        early = jnp.zeros((wins * cols, 2 * c2), F32)
        now = [early, early]
        for i in range(2):
            lhs = [mcat[f, i : i + wins, :, lanes].reshape(wins * cols, 2 * c1) for f in range(2)]
            early = early + dot(lhs[0], v2[0, b, i])
            for f in range(2):
                now[f] = now[f] + dot(lhs[f], v2[1, b, i])
        for f in range(2):
            total = early + now[f]
            for w in range(wins):
                for a in range(2):
                    v = total[w * cols : (w + 1) * cols, a * c2 : (a + 1) * c2] + bias
                    v = silu(v)
                    if w == 0 and a == 0:
                        v = jnp.where(first_tile, 0.0, v)
                    if w == wins - 1 and a == 1:
                        v = jnp.where(last_tile, 0.0, v)
                    before, after = shifted(v)
                    r = 2 * w + a
                    if b == 0:
                        lcat[f, r, :, 0:c2] = before.astype(BF16)
                        lcat[f, r, :, 2 * c2 : 3 * c2] = v.astype(BF16)
                    else:
                        lcat[f, r, :, c2 : 2 * c2] = v.astype(BF16)
                        lcat[f, r, :, 3 * c2 : 4 * c2] = after.astype(BF16)

    lrows = 2 * wins
    wins = lrows - 1
    bias = b3[...].astype(F32)[None, :]
    for q in range(4):
        b = 1 if q % 2 == 0 else 0
        at = (0, c2, c2, 2 * c2)[q]
        total = jnp.zeros((wins * cols, 2 * c3), F32)
        for i in range(2):
            for f in range(2):
                lhs = lcat[f, i : i + wins, :, at : at + 2 * c2].reshape(wins * cols, 2 * c2)
                total = total + dot(lhs, v3[f, b, i])
        for o in range(4 * rows):
            a = 1 - o % 2
            w = (o + 1) // 2
            v = total[w * cols : (w + 1) * cols, a * c3 : (a + 1) * c3] + bias
            wide[o, pl.ds(q, cols, stride=4), :] = v
    for o in range(4 * rows):
        out[o] = wide[o].astype(BF16)


def in_vmem(x):
    return pltpu.with_memory_space_constraint(x, pltpu.VMEM)


def per_device(features, conv_first, bias_first, conv_second, bias_second, conv_third, bias_third):
    own = features[0]
    rows, cols, c1 = own.shape
    c2 = conv_second.shape[4]
    c3 = conv_third.shape[4]
    tiles = lax.axis_size("tile")
    swap = [(0, 1), (1, 0)]
    apart = [(i, tiles + i + 1) for i in range(tiles - 1)]
    apart += [(tiles + i + 1, i) for i in range(tiles - 1)]
    vmem = pl.BlockSpec(memory_space=pltpu.VMEM)
    anywhere = pl.BlockSpec(memory_space=pl.ANY)

    other = lax.ppermute(own, "sect", swap)
    pair = pl.pallas_call(
        pair_kernel,
        out_shape=pltpu.VMEM((2, rows, cols, c1), BF16),
        in_specs=[vmem] * 2,
        out_specs=vmem,
        cost_estimate=pl.CostEstimate(flops=12_000_000_000, bytes_accessed=1024, transcendentals=0),
        compiler_params=pltpu.CompilerParams(vmem_limit_bytes=1 << 20),
    )(in_vmem(own), in_vmem(other))
    if rows == 2:
        edge = pair
    else:
        edge = jnp.where(lax.axis_index("sect") == 0, pair[:, rows - 2 :], pair[:, :2])
    far = lax.ppermute(edge, ("sect", "tile"), apart)
    near = lax.ppermute(far, "sect", swap)
    acc, v1, wn, v2, v3 = pl.pallas_call(
        early_kernel,
        out_shape=[
            pltpu.VMEM((2, rows + 2, cols, c1), F32),
            pltpu.VMEM((3, 3 * c1, c1), BF16),
            pltpu.VMEM((3, 3, c1, c1), BF16),
            pltpu.VMEM((2, 2, 2, 2 * c1, 2 * c2), BF16),
            pltpu.VMEM((2, 2, 2, 2 * c2, 2 * c3), BF16),
        ],
        in_specs=[vmem, anywhere, vmem, vmem],
        out_specs=[vmem] * 5,
        scratch_shapes=[
            pltpu.VMEM((2, rows, cols, 3 * c1), BF16),
            pltpu.VMEM((3, 2, 3, c1, c1), BF16),
            pltpu.SemaphoreType.DMA((3, 3)),
        ],
        cost_estimate=pl.CostEstimate(flops=6_000_000_000, bytes_accessed=1024, transcendentals=0),
        compiler_params=pltpu.CompilerParams(vmem_limit_bytes=16 << 20),
    )(
        in_vmem(pair),
        pltpu.with_memory_space_constraint(conv_first, pltpu.HBM),
        in_vmem(conv_second),
        in_vmem(conv_third),
    )
    out = pl.pallas_call(
        late_kernel,
        out_shape=jax.ShapeDtypeStruct((4 * rows, 4 * cols, c3), BF16),
        in_specs=[vmem] * 11,
        out_specs=vmem,
        scratch_shapes=[
            pltpu.VMEM((2, 4, cols, 3 * c1), BF16),
            pltpu.VMEM((2, rows + 2, cols, 3 * c1), BF16),
            pltpu.VMEM((2, 2 * rows + 2, cols, 4 * c2), BF16),
            pltpu.VMEM((4 * rows, 4 * cols, c3), F32),
        ],
        cost_estimate=pl.CostEstimate(flops=8_000_000_000, bytes_accessed=1024, transcendentals=0),
        compiler_params=pltpu.CompilerParams(vmem_limit_bytes=14 << 20),
    )(
        in_vmem(pair),
        in_vmem(far),
        in_vmem(near),
        in_vmem(acc),
        in_vmem(v1),
        in_vmem(wn),
        bias_first,
        in_vmem(v2),
        bias_second,
        in_vmem(v3),
        bias_third,
    )
    return out[None]


def solution(mesh):
    return jax.shard_map(
        per_device,
        mesh=mesh,
        in_specs=(P(("groups", "sect"), "tile", None, None), P(), P(), P(), P(), P(), P()),
        out_specs=P(("groups", "sect"), "tile", None, None),
        check_vma=False,
    )
```

```python
import jax
import jax.numpy as jnp
from jax import lax
from jax.experimental import pallas as pl
from jax.experimental.pallas import tpu as pltpu
from jax.sharding import PartitionSpec as P

F32 = jnp.float32
BF16 = jnp.bfloat16


def silu(v):
    half = 0.5 * v
    return half + half * jnp.tanh(half)


def shifted(v):
    count = v.shape[0]
    column = lax.broadcasted_iota(jnp.int32, v.shape, 0)
    before = jnp.where(column == 0, 0.0, pltpu.roll(v, 1, 0))
    after = jnp.where(column == count - 1, 0.0, pltpu.roll(v, count - 1, 0))
    return before, after


def dot(a, b):
    return jnp.dot(a, b, preferred_element_type=F32)


def merge_time(source, target):
    cin = source.shape[2]
    step = 64

    def body(n, _):
        at = pl.multiple_of(n * step, step)
        for j in range(3):
            total = source[0, j, pl.ds(at, step), :] + source[1, j, pl.ds(at, step), :]
            target[pl.ds(j * cin + at, step), :] = total
        return 0

    lax.fori_loop(0, cin // step, body, 0)


def merge_space(source, target, step):
    cin, cout = source.shape[3], source.shape[4]

    def body(n, _):
        at = pl.multiple_of(n * step, step)
        for t in range(2):
            tap = {}
            for i in range(3):
                for j in range(3):
                    if t == 0:
                        tap[i, j] = source[0, i, j, pl.ds(at, step), :].astype(F32) + source[
                            1, i, j, pl.ds(at, step), :
                        ].astype(F32)
                    else:
                        tap[i, j] = source[2, i, j, pl.ds(at, step), :].astype(F32)
            for a in range(2):
                for i in range(2):
                    if a == i:
                        lo = i
                        row = [tap[lo, j] + tap[lo + 1, j] for j in range(3)]
                    else:
                        row = [tap[2 * i, j] for j in range(3)]
                    for b in range(2):
                        if b == 0:
                            columns = (row[0] + row[1], row[2])
                        else:
                            columns = (row[0], row[1] + row[2])
                        for j in range(2):
                            target[t, b, i, pl.ds(j * cin + at, step), pl.ds(a * cout, cout)] = columns[
                                j
                            ].astype(BF16)
        return 0

    lax.fori_loop(0, cin // step, body, 0)


def put_cat(target, at, v):
    chans = v.shape[1]
    before, after = shifted(v)
    target[(*at, slice(None), slice(0, chans))] = before.astype(BF16)
    target[(*at, slice(None), slice(chans, 2 * chans))] = v.astype(BF16)
    target[(*at, slice(None), slice(2 * chans, 3 * chans))] = after.astype(BF16)


def load_kernel(own, pair, sem):
    copy = pltpu.make_async_copy(own, pair.at[0], sem)
    copy.start()
    copy.wait()


def pair_kernel(half, other, pair):
    pair[1] = other[...]


def halo_part(source, at, upper, acc, v1, wn, cat):
    cols, c1 = source.shape[2:]
    rows = acc.shape[1] - 3
    size = 2 * cols
    for f in range(2):
        for r in range(2):
            put_cat(cat, (f, r), silu(source[at[f], r].astype(F32)))

    def tap(k, _):
        middle = k == 1
        i = jnp.where(middle, 1, jnp.where(upper, 0, 2))
        both = cat[...].reshape(2 * size, 3 * c1)
        part = dot(both[:size], v1[i])
        total = dot(both, wn[i].reshape(3 * c1, c1))
        m = [
            jnp.where(middle, jnp.where(upper, rows + 2, rows + 1), jnp.where(upper, 0, rows)),
            jnp.where(middle, jnp.where(upper, 0, rows + 2), jnp.where(upper, 1, rows + 1)),
        ]
        for f in range(2):
            value = (total[f * size : (f + 1) * size] + part).reshape(2, cols, c1)
            for r in range(2):
                acc[f, m[r]] += value[r]
        return 0

    lax.fori_loop(0, 2, tap, 0)


def early_kernel(pair, w1, w2, w3, acc, v1, wn, v2, v3, cat, raw, sems):
    rows, cols, c1 = pair.shape[1:]
    second = lax.axis_index("sect") > 0

    def copy(t, i):
        target = raw.at[i, t] if t < 2 else wn.at[i]
        return pltpu.make_async_copy(w1.at[t, i], target, sems.at[i, t])

    for i in range(3):
        for t in range(3):
            copy(t, i).start()
    for r in range(rows):
        mine, other = pair[0, r].astype(F32), pair[1, r].astype(F32)
        put_cat(cat, (0, r), silu(jnp.where(second, other, mine)))
        put_cat(cat, (1, r), silu(mine))
    merge_space(w3, v3, 16)
    merge_space(w2, v2, 16)
    size = rows * cols
    acc[...] = jnp.zeros(acc.shape, F32)

    def tap(i, _):
        for t in range(3):
            copy(t, i).wait()
        merge_time(raw.at[i], v1.at[i])
        both = cat[...].reshape(2 * size, 3 * c1)
        part = dot(both[:size], v1[i])
        total = dot(both, wn[i].reshape(3 * c1, c1))
        for f in range(2):
            value = (total[f * size : (f + 1) * size] + part).reshape(rows, cols, c1)
            acc[f, pl.ds(2 - i, rows)] += value
        return 0

    lax.fori_loop(0, 3, tap, 0)


def middle_kernel(far, before, v1, wn, acc, cat):
    second = lax.axis_index("sect") > 0
    halo_part(far, (jnp.where(second, 0, 1), 1), second, acc, v1, wn, cat)


def late_kernel(
    pair, far, near, before, v1, wn, b1, v2, b2, v3, b3, out, acc, hcat, mcat, lcat, wide
):
    rows, cols, c1 = pair.shape[1:]
    c2 = b2.shape[0]
    c3 = b3.shape[0]
    second = lax.axis_index("sect") > 0
    tile = lax.axis_index("tile")
    first_tile = tile == 0
    last_tile = tile == lax.axis_size("tile") - 1

    def feature(f, r):
        if r < 2:
            if f == 0:
                return jnp.where(second, far[0, r].astype(F32), near[0, r].astype(F32))
            return jnp.where(second, far[1, r].astype(F32), near[0, r].astype(F32))
        if r < rows + 2:
            mine = pair[0, r - 2].astype(F32)
            if f == 1:
                return mine
            return jnp.where(second, pair[1, r - 2].astype(F32), mine)
        r = r - rows - 2
        if f == 0:
            return jnp.where(second, near[1, r].astype(F32), far[1, r].astype(F32))
        return jnp.where(second, near[0, r].astype(F32), far[1, r].astype(F32))

    mrows = rows + 2
    halo_part(near, (jnp.where(second, 1, 0), 0), jnp.logical_not(second), acc, v1, wn, hcat)
    bias = b1[...].astype(F32)[None, :]
    for f in range(2):
        for m in range(mrows):
            v = acc[f, m] + bias + feature(f, m + 1)
            v = silu(v.astype(BF16).astype(F32))
            if m == 0:
                v = jnp.where(first_tile, 0.0, v)
            if m == mrows - 1:
                v = jnp.where(last_tile, 0.0, v)
            put_cat(mcat, (f, m), v)

    wins = mrows - 1
    bias = b2[...].astype(F32)[None, :]
    for b in range(2):
        lanes = slice(c1, 3 * c1) if b == 0 else slice(0, 2 * c1)
        early = jnp.zeros((wins * cols, 2 * c2), F32)
        now = [early, early]
        for i in range(2):
            lhs = [mcat[f, i : i + wins, :, lanes].reshape(wins * cols, 2 * c1) for f in range(2)]
            early = early + dot(lhs[0], v2[0, b, i])
            for f in range(2):
                now[f] = now[f] + dot(lhs[f], v2[1, b, i])
        for f in range(2):
            total = early + now[f]
            for w in range(wins):
                for a in range(2):
                    v = total[w * cols : (w + 1) * cols, a * c2 : (a + 1) * c2] + bias
                    v = silu(v)
                    if w == 0 and a == 0:
                        v = jnp.where(first_tile, 0.0, v)
                    if w == wins - 1 and a == 1:
                        v = jnp.where(last_tile, 0.0, v)
                    before, after = shifted(v)
                    r = 2 * w + a
                    if b == 0:
                        lcat[f, r, :, 0:c2] = before.astype(BF16)
                        lcat[f, r, :, 2 * c2 : 3 * c2] = v.astype(BF16)
                    else:
                        lcat[f, r, :, c2 : 2 * c2] = v.astype(BF16)
                        lcat[f, r, :, 3 * c2 : 4 * c2] = after.astype(BF16)

    lrows = 2 * wins
    wins = lrows - 1
    bias = b3[...].astype(F32)[None, :]
    for q in range(4):
        b = 1 if q % 2 == 0 else 0
        at = (0, c2, c2, 2 * c2)[q]
        total = jnp.zeros((wins * cols, 2 * c3), F32)
        for i in range(2):
            for f in range(2):
                lhs = lcat[f, i : i + wins, :, at : at + 2 * c2].reshape(wins * cols, 2 * c2)
                total = total + dot(lhs, v3[f, b, i])
        for o in range(4 * rows):
            a = 1 - o % 2
            w = (o + 1) // 2
            v = total[w * cols : (w + 1) * cols, a * c3 : (a + 1) * c3] + bias
            wide[o, pl.ds(q, cols, stride=4), :] = v
    for o in range(4 * rows):
        out[o] = wide[o].astype(BF16)


def in_vmem(x):
    return pltpu.with_memory_space_constraint(x, pltpu.VMEM)


def per_device(features, conv_first, bias_first, conv_second, bias_second, conv_third, bias_third):
    own = features[0]
    rows, cols, c1 = own.shape
    c2 = conv_second.shape[4]
    c3 = conv_third.shape[4]
    tiles = lax.axis_size("tile")
    swap = [(0, 1), (1, 0)]
    apart = [(i, tiles + i + 1) for i in range(tiles - 1)]
    apart += [(tiles + i + 1, i) for i in range(tiles - 1)]
    vmem = pl.BlockSpec(memory_space=pltpu.VMEM)
    anywhere = pl.BlockSpec(memory_space=pl.ANY)

    other = lax.ppermute(own, "sect", swap)
    pair_shape = pltpu.VMEM((2, rows, cols, c1), BF16)
    half = pl.pallas_call(
        load_kernel,
        out_shape=pair_shape,
        in_specs=[anywhere],
        out_specs=vmem,
        scratch_shapes=[pltpu.SemaphoreType.DMA],
        cost_estimate=pl.CostEstimate(flops=6_000_000_000, bytes_accessed=1024, transcendentals=0),
        compiler_params=pltpu.CompilerParams(vmem_limit_bytes=1 << 20),
    )(pltpu.with_memory_space_constraint(own, pltpu.HBM))
    pair = pl.pallas_call(
        pair_kernel,
        out_shape=pair_shape,
        in_specs=[vmem] * 2,
        out_specs=vmem,
        input_output_aliases={0: 0},
        cost_estimate=pl.CostEstimate(flops=6_000_000_000, bytes_accessed=1024, transcendentals=0),
        compiler_params=pltpu.CompilerParams(vmem_limit_bytes=1 << 20),
    )(in_vmem(half), in_vmem(other))
    if rows == 2:
        edge = pair
    else:
        edge = jnp.where(lax.axis_index("sect") == 0, pair[:, rows - 2 :], pair[:, :2])
    far = lax.ppermute(edge, ("sect", "tile"), apart)
    near = lax.ppermute(far, "sect", swap)
    acc, v1, wn, v2, v3 = pl.pallas_call(
        early_kernel,
        out_shape=[
            pltpu.VMEM((2, rows + 3, cols, c1), F32),
            pltpu.VMEM((3, 3 * c1, c1), BF16),
            pltpu.VMEM((3, 3, c1, c1), BF16),
            pltpu.VMEM((2, 2, 2, 2 * c1, 2 * c2), BF16),
            pltpu.VMEM((2, 2, 2, 2 * c2, 2 * c3), BF16),
        ],
        in_specs=[vmem, anywhere, vmem, vmem],
        out_specs=[vmem] * 5,
        scratch_shapes=[
            pltpu.VMEM((2, rows, cols, 3 * c1), BF16),
            pltpu.VMEM((3, 2, 3, c1, c1), BF16),
            pltpu.SemaphoreType.DMA((3, 3)),
        ],
        cost_estimate=pl.CostEstimate(flops=6_000_000_000, bytes_accessed=1024, transcendentals=0),
        compiler_params=pltpu.CompilerParams(vmem_limit_bytes=16 << 20),
    )(
        in_vmem(pair),
        pltpu.with_memory_space_constraint(conv_first, pltpu.HBM),
        in_vmem(conv_second),
        in_vmem(conv_third),
    )
    acc_shape = pltpu.VMEM((2, rows + 3, cols, c1), F32)
    acc = pl.pallas_call(
        middle_kernel,
        out_shape=acc_shape,
        in_specs=[vmem] * 4,
        out_specs=vmem,
        input_output_aliases={1: 0},
        scratch_shapes=[pltpu.VMEM((2, 2, cols, 3 * c1), BF16)],
        cost_estimate=pl.CostEstimate(flops=2_000_000_000, bytes_accessed=1024, transcendentals=0),
        compiler_params=pltpu.CompilerParams(vmem_limit_bytes=8 << 20),
    )(in_vmem(far), in_vmem(acc), in_vmem(v1), in_vmem(wn))
    out, _ = pl.pallas_call(
        late_kernel,
        out_shape=[jax.ShapeDtypeStruct((4 * rows, 4 * cols, c3), BF16), acc_shape],
        in_specs=[vmem] * 11,
        out_specs=[vmem] * 2,
        input_output_aliases={3: 1},
        scratch_shapes=[
            pltpu.VMEM((2, 2, cols, 3 * c1), BF16),
            pltpu.VMEM((2, rows + 2, cols, 3 * c1), BF16),
            pltpu.VMEM((2, 2 * rows + 2, cols, 4 * c2), BF16),
            pltpu.VMEM((4 * rows, 4 * cols, c3), F32),
        ],
        cost_estimate=pl.CostEstimate(flops=8_000_000_000, bytes_accessed=1024, transcendentals=0),
        compiler_params=pltpu.CompilerParams(vmem_limit_bytes=14 << 20),
    )(
        in_vmem(pair),
        in_vmem(far),
        in_vmem(near),
        in_vmem(acc),
        in_vmem(v1),
        in_vmem(wn),
        bias_first,
        in_vmem(v2),
        bias_second,
        in_vmem(v3),
        bias_third,
    )
    return out[None]


def solution(mesh):
    return jax.shard_map(
        per_device,
        mesh=mesh,
        in_specs=(P(("groups", "sect"), "tile", None, None), P(), P(), P(), P(), P(), P()),
        out_specs=P(("groups", "sect"), "tile", None, None),
        check_vma=False,
    )
```

```python
import jax
import jax.numpy as jnp
from jax import lax
from jax.experimental import pallas as pl
from jax.experimental.pallas import tpu as pltpu
from jax.sharding import PartitionSpec as P

F32 = jnp.float32
BF16 = jnp.bfloat16


def silu(v):
    half = 0.5 * v
    return half + half * jnp.tanh(half)


def shifted(v):
    count = v.shape[0]
    column = lax.broadcasted_iota(jnp.int32, v.shape, 0)
    before = jnp.where(column == 0, 0.0, pltpu.roll(v, 1, 0))
    after = jnp.where(column == count - 1, 0.0, pltpu.roll(v, count - 1, 0))
    return before, after


def column_before(v):
    column = lax.broadcasted_iota(jnp.int32, v.shape, 0)
    return jnp.where(column == 0, 0.0, pltpu.roll(v, 1, 0))


def column_after(v, last):
    count = v.shape[0]
    column = lax.broadcasted_iota(jnp.int32, v.shape, 0)
    return jnp.where(column == count - 1, last, pltpu.roll(v, count - 1, 0))


def dot(a, b):
    return jnp.dot(a, b, preferred_element_type=F32)


def merge_time(source, target):
    cin = source.shape[2]
    step = 64

    def body(n, _):
        at = pl.multiple_of(n * step, step)
        for j in range(3):
            total = source[0, j, pl.ds(at, step), :] + source[1, j, pl.ds(at, step), :]
            target[pl.ds(j * cin + at, step), :] = total
        return 0

    lax.fori_loop(0, cin // step, body, 0)


ORDER = (0, 2, 1)


def merge_second(source, target):
    cin = source.shape[3]
    step = 64

    def body(n, _):
        at = pl.multiple_of(n * step, step)
        for i in range(3):
            for place, j in enumerate(ORDER):
                rows = pl.ds(place * cin + at, step)
                target[0, i, rows, :] = source[0, i, j, pl.ds(at, step), :] + source[1, i, j, pl.ds(at, step), :]
                target[1, i, rows, :] = source[2, i, j, pl.ds(at, step), :]
        return 0

    lax.fori_loop(0, cin // step, body, 0)


def merge_third(source, target):
    cin, cout = source.shape[3], source.shape[4]
    step = 32

    def body(n, _):
        at = pl.multiple_of(n * step, step)
        for t in range(2):
            for place, j in enumerate(ORDER):
                if t == 0:
                    tap = [
                        source[0, i, j, pl.ds(at, step), :].astype(F32)
                        + source[1, i, j, pl.ds(at, step), :].astype(F32)
                        for i in range(3)
                    ]
                else:
                    tap = [source[2, i, j, pl.ds(at, step), :].astype(F32) for i in range(3)]
                rows = pl.ds(place * cin + at, step)
                target[t, 0, rows, 0:cout] = (tap[0] + tap[1]).astype(BF16)
                target[t, 0, rows, cout : 2 * cout] = tap[0].astype(BF16)
                target[t, 1, rows, 0:cout] = tap[2].astype(BF16)
                target[t, 1, rows, cout : 2 * cout] = (tap[1] + tap[2]).astype(BF16)
        return 0

    lax.fori_loop(0, cin // step, body, 0)


def put_cat(target, at, v):
    chans = v.shape[1]
    before, after = shifted(v)
    target[(*at, slice(None), slice(0, chans))] = before.astype(BF16)
    target[(*at, slice(None), slice(chans, 2 * chans))] = v.astype(BF16)
    target[(*at, slice(None), slice(2 * chans, 3 * chans))] = after.astype(BF16)


def load_kernel(own, pair, sem):
    copy = pltpu.make_async_copy(own, pair.at[0], sem)
    copy.start()
    copy.wait()


def pair_kernel(half, other, pair):
    pair[1] = other[...]


def halo_part(source, at, upper, acc, v1, wn, cat):
    cols, c1 = source.shape[2:]
    rows = acc.shape[1] - 3
    size = 2 * cols
    for f in range(2):
        for r in range(2):
            put_cat(cat, (f, r), silu(source[at[f], r].astype(F32)))

    def tap(k, _):
        middle = k == 1
        i = jnp.where(middle, 1, jnp.where(upper, 0, 2))
        both = cat[...].reshape(2 * size, 3 * c1)
        part = dot(both[:size], v1[i])
        total = dot(both, wn[i].reshape(3 * c1, c1))
        m = [
            jnp.where(middle, jnp.where(upper, rows + 2, rows + 1), jnp.where(upper, 0, rows)),
            jnp.where(middle, jnp.where(upper, 0, rows + 2), jnp.where(upper, 1, rows + 1)),
        ]
        for f in range(2):
            value = (total[f * size : (f + 1) * size] + part).reshape(2, cols, c1)
            for r in range(2):
                acc[f, m[r]] += value[r]
        return 0

    lax.fori_loop(0, 2, tap, 0)


def early_kernel(pair, w1, w2, w3, acc, v1, wn, v2, v3, cat, raw, sems):
    rows, cols, c1 = pair.shape[1:]
    second = lax.axis_index("sect") > 0

    def copy(t, i):
        target = raw.at[i, t] if t < 2 else wn.at[i]
        return pltpu.make_async_copy(w1.at[t, i], target, sems.at[i, t])

    for i in range(3):
        for t in range(3):
            copy(t, i).start()
    for r in range(rows):
        mine, other = pair[0, r].astype(F32), pair[1, r].astype(F32)
        put_cat(cat, (0, r), silu(jnp.where(second, other, mine)))
        put_cat(cat, (1, r), silu(mine))
    merge_third(w3, v3)
    merge_second(w2, v2)
    size = rows * cols
    acc[...] = jnp.zeros(acc.shape, F32)

    def tap(i, _):
        for t in range(3):
            copy(t, i).wait()
        merge_time(raw.at[i], v1.at[i])
        both = cat[...].reshape(2 * size, 3 * c1)
        part = dot(both[:size], v1[i])
        total = dot(both, wn[i].reshape(3 * c1, c1))
        for f in range(2):
            value = (total[f * size : (f + 1) * size] + part).reshape(rows, cols, c1)
            acc[f, pl.ds(2 - i, rows)] += value
        return 0

    lax.fori_loop(0, 3, tap, 0)


def middle_kernel(far, before, v1, wn, acc, cat):
    second = lax.axis_index("sect") > 0
    halo_part(far, (jnp.where(second, 0, 1), 1), second, acc, v1, wn, cat)


def late_kernel(
    pair, far, near, before, v1, wn, b1, v2, b2, v3, b3, out, acc, hcat, mcat, medge, lcat, ledge, wide, so, si, uo, ui, po, pi
):
    rows, cols, c1 = pair.shape[1:]
    c2 = b2.shape[0]
    c3 = b3.shape[0]
    second = lax.axis_index("sect") > 0
    tile = lax.axis_index("tile")
    first_tile = tile == 0
    last_tile = tile == lax.axis_size("tile") - 1

    def feature(f, r):
        if r < 2:
            if f == 0:
                return jnp.where(second, far[0, r].astype(F32), near[0, r].astype(F32))
            return jnp.where(second, far[1, r].astype(F32), near[0, r].astype(F32))
        if r < rows + 2:
            mine = pair[0, r - 2].astype(F32)
            if f == 1:
                return mine
            return jnp.where(second, pair[1, r - 2].astype(F32), mine)
        r = r - rows - 2
        if f == 0:
            return jnp.where(second, near[1, r].astype(F32), far[1, r].astype(F32))
        return jnp.where(second, near[0, r].astype(F32), far[1, r].astype(F32))

    mrows = rows + 2
    halo_part(near, (jnp.where(second, 1, 0), 0), jnp.logical_not(second), acc, v1, wn, hcat)
    bias = b1[...].astype(F32)[None, :]
    medge[...] = jnp.zeros(medge.shape, F32)
    for f in range(2):
        for m in range(mrows):
            v = acc[f, m] + bias + feature(f, m + 1)
            v = silu(v.astype(BF16).astype(F32))
            if m == 0:
                v = jnp.where(first_tile, 0.0, v)
            if m == mrows - 1:
                v = jnp.where(last_tile, 0.0, v)
            mcat[f, m, :, 0:c1] = column_before(v).astype(BF16)
            mcat[f, m, :, c1 : 2 * c1] = v.astype(BF16)
            medge[f, m : m + 1, 0:c1] = v[cols - 1 : cols]

    wins = mrows - 1
    size = wins * cols

    def products(t, i, first, count, frames):
        pieces, singles = [], []
        for f in range(frames):
            pieces.append(mcat[f, pl.ds(first, count)].reshape(count * cols, 2 * c1))
            pieces.append(medge[f].astype(BF16))
            singles.append(mcat[f, pl.ds(first, count), :, c1 : 2 * c1].reshape(count * cols, c1))
        outer = dot(jnp.concatenate(pieces, axis=0), v2[t, i, 0 : 2 * c1])
        inner = dot(jnp.concatenate(singles, axis=0), v2[t, i, 2 * c1 : 3 * c1])
        return outer, inner

    def around(k, _):
        so[k, 0, 0 : size + 16], si[k, 0, 0:size] = products(0, 2 * k, k, wins, 1)
        so[k, 1], si[k, 1] = products(1, 2 * k, k, wins, 2)
        return 0

    lax.fori_loop(0, 2, around, 0)

    def centre(k, _):
        uo[0, 0 : size + cols + 16], ui[0, 0 : size + cols] = products(0, 1, k, mrows, 1)
        uo[1], ui[1] = products(1, 1, k, mrows, 2)
        return 0

    lax.fori_loop(0, 1, centre, 0)
    bias = b2[...].astype(F32)[None, :]
    ledge[...] = jnp.zeros(ledge.shape, F32)
    for f in range(2):
        for w in range(wins):

            def around_at(ref, at, count, stride):
                total = 0.0
                for k in range(2):
                    row = at + (k if count == 1 else 0)
                    total = total + ref[k, 0, row : row + count] + ref[k, 1, f * stride + row : f * stride + row + count]
                return total

            def centre_at(ref, at, count, stride):
                return ref[0, at : at + count] + ref[1, f * stride + at : f * stride + at + count]

            outer = around_at(so, w * cols, cols, size + 16)
            inner = around_at(si, w * cols, cols, size)
            edge = around_at(so, size + w, 1, size + 16)
            full = mrows * cols
            for a in range(2):
                up = outer + centre_at(uo, (w + a) * cols, cols, full + 16)
                mid = inner + centre_at(ui, (w + a) * cols, cols, full) + bias
                last = edge + centre_at(uo, full + w + a, 1, full + 16)
                even = silu(up + mid)
                odd = silu(column_after(up, last) + mid)
                if w == 0 and a == 0:
                    even, odd = jnp.where(first_tile, 0.0, even), jnp.where(first_tile, 0.0, odd)
                if w == wins - 1 and a == 1:
                    even, odd = jnp.where(last_tile, 0.0, even), jnp.where(last_tile, 0.0, odd)
                r = 2 * w + a
                lcat[f, r, :, 0:c2] = column_before(odd).astype(BF16)
                lcat[f, r, :, c2 : 2 * c2] = even.astype(BF16)
                lcat[f, r, :, 2 * c2 : 3 * c2] = odd.astype(BF16)
                ledge[f, r : r + 1, 0:c2] = odd[cols - 1 : cols]

    wins = 2 * wins - 1
    size = wins * cols
    bias = b3[...].astype(F32)[None, :]

    def pairs_of(k, _):
        for f in range(2):
            rows_of = lcat[f, pl.ds(k, wins)].reshape(size, 3 * c2)
            pairs = jnp.concatenate(
                [rows_of[:, 0 : 2 * c2], rows_of[:, c2 : 3 * c2], ledge[f].astype(BF16)], axis=0
            )
            po[f, k] = dot(pairs, v3[f, k, 0 : 2 * c2])
            single = jnp.concatenate([rows_of[:, c2 : 2 * c2], rows_of[:, 2 * c2 : 3 * c2]], axis=0)
            pi[f, k] = dot(single, v3[f, k, 2 * c2 : 3 * c2])
        return 0

    lax.fori_loop(0, 2, pairs_of, 0)
    for o in range(4 * rows):
        a = 1 - o % 2
        w = (o + 1) // 2
        lanes = slice(a * c3, (a + 1) * c3)

        def cell(ref, at):
            here = slice(at * cols, (at + 1) * cols)
            return ref[0, 0, here, lanes] + ref[0, 1, here, lanes] + ref[1, 0, here, lanes] + ref[1, 1, here, lanes]

        apart = cell(po, w)
        close = cell(po, wins + w)
        last = 0.0
        for f in range(2):
            for k in range(2):
                row = 2 * size + w + k
                last = last + po[f, k, row : row + 1, lanes]
        even = cell(pi, w) + bias
        odd = cell(pi, wins + w) + bias
        for q, v in enumerate((apart + even, close + even, close + odd, column_after(apart, last) + odd)):
            wide[o, pl.ds(q, cols, stride=4), :] = v
        out[o] = wide[o].astype(BF16)


def in_vmem(x):
    return pltpu.with_memory_space_constraint(x, pltpu.VMEM)


def per_device(features, conv_first, bias_first, conv_second, bias_second, conv_third, bias_third):
    own = features[0]
    rows, cols, c1 = own.shape
    c2 = conv_second.shape[4]
    c3 = conv_third.shape[4]
    tiles = lax.axis_size("tile")
    swap = [(0, 1), (1, 0)]
    apart = [(i, tiles + i + 1) for i in range(tiles - 1)]
    apart += [(tiles + i + 1, i) for i in range(tiles - 1)]
    vmem = pl.BlockSpec(memory_space=pltpu.VMEM)
    anywhere = pl.BlockSpec(memory_space=pl.ANY)

    other = lax.ppermute(own, "sect", swap)
    pair_shape = pltpu.VMEM((2, rows, cols, c1), BF16)
    half = pl.pallas_call(
        load_kernel,
        out_shape=pair_shape,
        in_specs=[anywhere],
        out_specs=vmem,
        scratch_shapes=[pltpu.SemaphoreType.DMA],
        cost_estimate=pl.CostEstimate(flops=6_000_000_000, bytes_accessed=1024, transcendentals=0),
        compiler_params=pltpu.CompilerParams(vmem_limit_bytes=1 << 20),
    )(pltpu.with_memory_space_constraint(own, pltpu.HBM))
    pair = pl.pallas_call(
        pair_kernel,
        out_shape=pair_shape,
        in_specs=[vmem] * 2,
        out_specs=vmem,
        input_output_aliases={0: 0},
        cost_estimate=pl.CostEstimate(flops=6_000_000_000, bytes_accessed=1024, transcendentals=0),
        compiler_params=pltpu.CompilerParams(vmem_limit_bytes=1 << 20),
    )(in_vmem(half), in_vmem(other))
    if rows == 2:
        edge = pair
    else:
        edge = jnp.where(lax.axis_index("sect") == 0, pair[:, rows - 2 :], pair[:, :2])
    far = lax.ppermute(edge, ("sect", "tile"), apart)
    near = lax.ppermute(far, "sect", swap)
    acc, v1, wn, v2, v3 = pl.pallas_call(
        early_kernel,
        out_shape=[
            pltpu.VMEM((2, rows + 3, cols, c1), F32),
            pltpu.VMEM((3, 3 * c1, c1), BF16),
            pltpu.VMEM((3, 3, c1, c1), BF16),
            pltpu.VMEM((2, 3, 3 * c1, c2), BF16),
            pltpu.VMEM((2, 2, 3 * c2, 2 * c3), BF16),
        ],
        in_specs=[vmem, anywhere, vmem, vmem],
        out_specs=[vmem] * 5,
        scratch_shapes=[
            pltpu.VMEM((2, rows, cols, 3 * c1), BF16),
            pltpu.VMEM((3, 2, 3, c1, c1), BF16),
            pltpu.SemaphoreType.DMA((3, 3)),
        ],
        cost_estimate=pl.CostEstimate(flops=6_000_000_000, bytes_accessed=1024, transcendentals=0),
        compiler_params=pltpu.CompilerParams(vmem_limit_bytes=16 << 20),
    )(
        in_vmem(pair),
        pltpu.with_memory_space_constraint(conv_first, pltpu.HBM),
        in_vmem(conv_second),
        in_vmem(conv_third),
    )
    acc_shape = pltpu.VMEM((2, rows + 3, cols, c1), F32)
    acc = pl.pallas_call(
        middle_kernel,
        out_shape=acc_shape,
        in_specs=[vmem] * 4,
        out_specs=vmem,
        input_output_aliases={1: 0},
        scratch_shapes=[pltpu.VMEM((2, 2, cols, 3 * c1), BF16)],
        cost_estimate=pl.CostEstimate(flops=2_000_000_000, bytes_accessed=1024, transcendentals=0),
        compiler_params=pltpu.CompilerParams(vmem_limit_bytes=8 << 20),
    )(in_vmem(far), in_vmem(acc), in_vmem(v1), in_vmem(wn))
    out, _ = pl.pallas_call(
        late_kernel,
        out_shape=[jax.ShapeDtypeStruct((4 * rows, 4 * cols, c3), BF16), acc_shape],
        in_specs=[vmem] * 11,
        out_specs=[vmem] * 2,
        input_output_aliases={3: 1},
        scratch_shapes=[
            pltpu.VMEM((2, 2, cols, 3 * c1), BF16),
            pltpu.VMEM((2, rows + 2, cols, 2 * c1), BF16),
            pltpu.VMEM((2, -(-(rows + 2) // 16) * 16, 2 * c1), F32),
            pltpu.VMEM((2, 2 * rows + 2, cols, 3 * c2), BF16),
            pltpu.VMEM((2, -(-(2 * rows + 2) // 16) * 16, 2 * c2), F32),
            pltpu.VMEM((4 * rows, 4 * cols, c3), F32),
            pltpu.VMEM((2, 2, 2 * ((rows + 1) * cols + 16), c2), F32),
            pltpu.VMEM((2, 2, 2 * (rows + 1) * cols, c2), F32),
            pltpu.VMEM((2, 2 * ((rows + 2) * cols + 16), c2), F32),
            pltpu.VMEM((2, 2 * (rows + 2) * cols, c2), F32),
            pltpu.VMEM((2, 2, 2 * (2 * rows + 1) * cols + 16, 2 * c3), F32),
            pltpu.VMEM((2, 2, 2 * (2 * rows + 1) * cols, 2 * c3), F32),
        ],
        cost_estimate=pl.CostEstimate(flops=8_000_000_000, bytes_accessed=1024, transcendentals=0),
        compiler_params=pltpu.CompilerParams(vmem_limit_bytes=24 << 20),
    )(
        in_vmem(pair),
        in_vmem(far),
        in_vmem(near),
        in_vmem(acc),
        in_vmem(v1),
        in_vmem(wn),
        bias_first,
        in_vmem(v2),
        bias_second,
        in_vmem(v3),
        bias_third,
    )
    return out[None]


def solution(mesh):
    return jax.shard_map(
        per_device,
        mesh=mesh,
        in_specs=(P(("groups", "sect"), "tile", None, None), P(), P(), P(), P(), P(), P()),
        out_specs=P(("groups", "sect"), "tile", None, None),
        check_vma=False,
    )
```

```python
import jax
import jax.numpy as jnp
from jax import lax
from jax.experimental import pallas as pl
from jax.experimental.pallas import tpu as pltpu
from jax.sharding import PartitionSpec as P

F32 = jnp.float32
BF16 = jnp.bfloat16


def silu(v):
    half = 0.5 * v
    return half + half * jnp.tanh(half)


def shifted(v):
    count = v.shape[0]
    column = lax.broadcasted_iota(jnp.int32, v.shape, 0)
    before = jnp.where(column == 0, 0.0, pltpu.roll(v, 1, 0))
    after = jnp.where(column == count - 1, 0.0, pltpu.roll(v, count - 1, 0))
    return before, after


def dot(a, b):
    return jnp.dot(a, b, preferred_element_type=F32)


def merge_time(source, target):
    cin = source.shape[2]
    step = 64

    def body(n, _):
        at = pl.multiple_of(n * step, step)
        for j in range(3):
            total = source[0, j, pl.ds(at, step), :] + source[1, j, pl.ds(at, step), :]
            target[pl.ds(j * cin + at, step), :] = total
        return 0

    lax.fori_loop(0, cin // step, body, 0)


def merge_space(source, target, step):
    cin, cout = source.shape[3], source.shape[4]

    def body(n, _):
        at = pl.multiple_of(n * step, step)
        for t in range(2):
            tap = {}
            for i in range(3):
                for j in range(3):
                    if t == 0:
                        tap[i, j] = source[0, i, j, pl.ds(at, step), :].astype(F32) + source[
                            1, i, j, pl.ds(at, step), :
                        ].astype(F32)
                    else:
                        tap[i, j] = source[2, i, j, pl.ds(at, step), :].astype(F32)
            for a in range(2):
                for i in range(2):
                    if a == i:
                        lo = i
                        row = [tap[lo, j] + tap[lo + 1, j] for j in range(3)]
                    else:
                        row = [tap[2 * i, j] for j in range(3)]
                    for b in range(2):
                        if b == 0:
                            columns = (row[0] + row[1], row[2])
                        else:
                            columns = (row[0], row[1] + row[2])
                        for j in range(2):
                            target[t, b, i, pl.ds(j * cin + at, step), pl.ds(a * cout, cout)] = columns[
                                j
                            ].astype(BF16)
        return 0

    lax.fori_loop(0, cin // step, body, 0)


def put_cat(target, at, v):
    chans = v.shape[1]
    before, after = shifted(v)
    target[(*at, slice(None), slice(0, chans))] = before.astype(BF16)
    target[(*at, slice(None), slice(chans, 2 * chans))] = v.astype(BF16)
    target[(*at, slice(None), slice(2 * chans, 3 * chans))] = after.astype(BF16)


def mark_kernel(other, out):
    pass


def halo_rows(i, rows):
    return jnp.where(i < 2, 0, rows), jnp.where(i < 1, 1, rows + 1)


def early_kernel(own, other, w1, w2, w3, mine, acc, v1, wn, v2, v3, cat, raw, sems, own_sem):
    rows, cols, c1 = other.shape
    second = lax.axis_index("sect") > 0

    def copy(t, i):
        target = raw.at[i, t] if t < 2 else wn.at[i]
        return pltpu.make_async_copy(w1.at[t, i], target, sems.at[i, t])

    load = pltpu.make_async_copy(own, mine, own_sem)
    load.start()
    for i in range(3):
        for t in range(3):
            copy(t, i).start()
    merge_space(w3, v3, 16)
    merge_space(w2, v2, 16)
    load.wait()
    for r in range(rows):
        v = mine[r].astype(F32)
        put_cat(cat, (0, r), silu(jnp.where(second, other[r].astype(F32), v)))
        put_cat(cat, (1, r), silu(v))
    size = rows * cols
    acc[...] = jnp.zeros(acc.shape, F32)

    def tap(i, _):
        for t in range(3):
            copy(t, i).wait()
        merge_time(raw.at[i], v1.at[i])
        both = cat[...].reshape(2 * size, 3 * c1)
        part = dot(both[:size], v1[i])
        total = dot(both, wn[i].reshape(3 * c1, c1))
        for f in range(2):
            value = (total[f * size : (f + 1) * size] + part).reshape(rows, cols, c1)
            acc[f, pl.ds(2 - i, rows)] += value
        return 0

    lax.fori_loop(0, 3, tap, 0)


def middle_kernel(halo, before, wn, acc, cat):
    cols, c1 = halo.shape[1:]
    rows = acc.shape[1] - 2
    for r in range(4):
        put_cat(cat, (r,), silu(halo[r].astype(F32)))

    def tap(i, _):
        lhs = cat[pl.ds(i, 2)].reshape(2 * cols, 3 * c1)
        value = dot(lhs, wn[i].reshape(3 * c1, c1)).reshape(2, cols, c1)
        for r, m in enumerate(halo_rows(i, rows)):
            acc[1, m] += value[r]
        return 0

    lax.fori_loop(0, 3, tap, 0)


def late_kernel(
    own, halo, own0, halo0, before, v1, wn, b1, v2, b2, v3, b3, out, acc, hcat, mcat, lcat, wide
):
    rows, cols, c1 = own.shape
    c2 = b2.shape[0]
    c3 = b3.shape[0]
    second = lax.axis_index("sect") > 0
    tile = lax.axis_index("tile")
    first_tile = tile == 0
    last_tile = tile == lax.axis_size("tile") - 1

    def feature(f, r):
        if r < 2:
            mine, other = halo[r], halo0[r]
        elif r < rows + 2:
            mine, other = own[r - 2], own0[r - 2]
        else:
            mine, other = halo[r - rows], halo0[r - rows]
        mine = mine.astype(F32)
        if f == 1:
            return mine
        return jnp.where(second, other.astype(F32), mine)

    mrows = rows + 2
    for r in range(4):
        put_cat(hcat, (r,), silu(feature(0, r if r < 2 else r + rows)))

    def tap(i, _):
        lhs = hcat[pl.ds(i, 2)].reshape(2 * cols, 3 * c1)
        part = dot(lhs, v1[i]).reshape(2, cols, c1)
        now = dot(lhs, wn[i].reshape(3 * c1, c1)).reshape(2, cols, c1)
        for r, m in enumerate(halo_rows(i, rows)):
            acc[0, m] += part[r] + now[r]
            acc[1, m] += part[r]
        return 0

    lax.fori_loop(0, 3, tap, 0)
    bias = b1[...].astype(F32)[None, :]
    for f in range(2):
        for m in range(mrows):
            v = acc[f, m] + bias + feature(f, m + 1)
            v = silu(v.astype(BF16).astype(F32))
            if m == 0:
                v = jnp.where(first_tile, 0.0, v)
            if m == mrows - 1:
                v = jnp.where(last_tile, 0.0, v)
            put_cat(mcat, (f, m), v)

    wins = mrows - 1
    bias = b2[...].astype(F32)[None, :]
    for b in range(2):
        lanes = slice(c1, 3 * c1) if b == 0 else slice(0, 2 * c1)
        early = jnp.zeros((wins * cols, 2 * c2), F32)
        now = [early, early]
        for i in range(2):
            lhs = [mcat[f, i : i + wins, :, lanes].reshape(wins * cols, 2 * c1) for f in range(2)]
            early = early + dot(lhs[0], v2[0, b, i])
            for f in range(2):
                now[f] = now[f] + dot(lhs[f], v2[1, b, i])
        for f in range(2):
            total = early + now[f]
            for w in range(wins):
                for a in range(2):
                    v = total[w * cols : (w + 1) * cols, a * c2 : (a + 1) * c2] + bias
                    v = silu(v)
                    if w == 0 and a == 0:
                        v = jnp.where(first_tile, 0.0, v)
                    if w == wins - 1 and a == 1:
                        v = jnp.where(last_tile, 0.0, v)
                    before, after = shifted(v)
                    r = 2 * w + a
                    if b == 0:
                        lcat[f, r, :, 0:c2] = before.astype(BF16)
                        lcat[f, r, :, 2 * c2 : 3 * c2] = v.astype(BF16)
                    else:
                        lcat[f, r, :, c2 : 2 * c2] = v.astype(BF16)
                        lcat[f, r, :, 3 * c2 : 4 * c2] = after.astype(BF16)

    lrows = 2 * wins
    wins = lrows - 1
    bias = b3[...].astype(F32)[None, :]
    for q in range(4):
        b = 1 if q % 2 == 0 else 0
        at = (0, c2, c2, 2 * c2)[q]
        total = jnp.zeros((wins * cols, 2 * c3), F32)
        for i in range(2):
            for f in range(2):
                lhs = lcat[f, i : i + wins, :, at : at + 2 * c2].reshape(wins * cols, 2 * c2)
                total = total + dot(lhs, v3[f, b, i])
        for o in range(4 * rows):
            a = 1 - o % 2
            w = (o + 1) // 2
            v = total[w * cols : (w + 1) * cols, a * c3 : (a + 1) * c3] + bias
            wide[o, pl.ds(q, cols, stride=4), :] = v
    for o in range(4 * rows):
        out[o] = wide[o].astype(BF16)


def in_vmem(x):
    return pltpu.with_memory_space_constraint(x, pltpu.VMEM)


def per_device(features, conv_first, bias_first, conv_second, bias_second, conv_third, bias_third):
    own = features[0]
    rows, cols, c1 = own.shape
    c2 = conv_second.shape[4]
    c3 = conv_third.shape[4]
    tiles = lax.axis_size("tile")
    forward = [(i, i + 1) for i in range(tiles - 1)]
    backward = [(i + 1, i) for i in range(tiles - 1)]
    across = [(0, 1)]
    vmem = pl.BlockSpec(memory_space=pltpu.VMEM)
    anywhere = pl.BlockSpec(memory_space=pl.ANY)
    acc_shape = pltpu.VMEM((2, rows + 2, cols, c1), F32)
    own_shape = pltpu.VMEM((rows, cols, c1), BF16)

    own0 = lax.ppermute(own, "sect", across)
    top = lax.ppermute(own[rows - 2 :], "tile", forward)
    bottom = lax.ppermute(own[:2], "tile", backward)
    own0 = pl.pallas_call(
        mark_kernel,
        out_shape=own_shape,
        in_specs=[vmem],
        out_specs=vmem,
        input_output_aliases={0: 0},
        cost_estimate=pl.CostEstimate(flops=12_000_000_000, bytes_accessed=1024, transcendentals=0),
        compiler_params=pltpu.CompilerParams(vmem_limit_bytes=1 << 20),
    )(in_vmem(own0))
    halo = jnp.concatenate([top, bottom], axis=0)
    halo0 = lax.ppermute(halo, "sect", across)
    mine, acc, v1, wn, v2, v3 = pl.pallas_call(
        early_kernel,
        out_shape=[
            own_shape,
            acc_shape,
            pltpu.VMEM((3, 3 * c1, c1), BF16),
            pltpu.VMEM((3, 3, c1, c1), BF16),
            pltpu.VMEM((2, 2, 2, 2 * c1, 2 * c2), BF16),
            pltpu.VMEM((2, 2, 2, 2 * c2, 2 * c3), BF16),
        ],
        in_specs=[anywhere, vmem, anywhere, vmem, vmem],
        out_specs=[vmem] * 6,
        scratch_shapes=[
            pltpu.VMEM((2, rows, cols, 3 * c1), BF16),
            pltpu.VMEM((3, 2, 3, c1, c1), BF16),
            pltpu.SemaphoreType.DMA((3, 3)),
            pltpu.SemaphoreType.DMA,
        ],
        cost_estimate=pl.CostEstimate(flops=6_000_000_000, bytes_accessed=1024, transcendentals=0),
        compiler_params=pltpu.CompilerParams(vmem_limit_bytes=16 << 20),
    )(
        pltpu.with_memory_space_constraint(own, pltpu.HBM),
        in_vmem(own0),
        pltpu.with_memory_space_constraint(conv_first, pltpu.HBM),
        in_vmem(conv_second),
        in_vmem(conv_third),
    )
    acc = pl.pallas_call(
        middle_kernel,
        out_shape=acc_shape,
        in_specs=[vmem] * 3,
        out_specs=vmem,
        input_output_aliases={1: 0},
        scratch_shapes=[pltpu.VMEM((4, cols, 3 * c1), BF16)],
        cost_estimate=pl.CostEstimate(flops=2_000_000_000, bytes_accessed=1024, transcendentals=0),
        compiler_params=pltpu.CompilerParams(vmem_limit_bytes=8 << 20),
    )(in_vmem(halo), in_vmem(acc), in_vmem(wn))
    out, _ = pl.pallas_call(
        late_kernel,
        out_shape=[jax.ShapeDtypeStruct((4 * rows, 4 * cols, c3), BF16), acc_shape],
        in_specs=[vmem] * 12,
        out_specs=[vmem] * 2,
        input_output_aliases={4: 1},
        scratch_shapes=[
            pltpu.VMEM((4, cols, 3 * c1), BF16),
            pltpu.VMEM((2, rows + 2, cols, 3 * c1), BF16),
            pltpu.VMEM((2, 2 * rows + 2, cols, 4 * c2), BF16),
            pltpu.VMEM((4 * rows, 4 * cols, c3), F32),
        ],
        cost_estimate=pl.CostEstimate(flops=8_000_000_000, bytes_accessed=1024, transcendentals=0),
        compiler_params=pltpu.CompilerParams(vmem_limit_bytes=14 << 20),
    )(
        in_vmem(mine),
        in_vmem(halo),
        in_vmem(own0),
        in_vmem(halo0),
        in_vmem(acc),
        in_vmem(v1),
        in_vmem(wn),
        bias_first,
        in_vmem(v2),
        bias_second,
        in_vmem(v3),
        bias_third,
    )
    return out[None]


def solution(mesh):
    return jax.shard_map(
        per_device,
        mesh=mesh,
        in_specs=(P(("groups", "sect"), "tile", None, None), P(), P(), P(), P(), P(), P()),
        out_specs=P(("groups", "sect"), "tile", None, None),
        check_vma=False,
    )
```

```python
import jax
import jax.numpy as jnp
from jax import lax
from jax.experimental import pallas as pl
from jax.experimental.pallas import tpu as pltpu
from jax.sharding import PartitionSpec as P

F32 = jnp.float32
BF16 = jnp.bfloat16


def silu(v):
    half = 0.5 * v
    return half + half * jnp.tanh(half)


def shifted(v):
    count = v.shape[0]
    column = lax.broadcasted_iota(jnp.int32, v.shape, 0)
    before = jnp.where(column == 0, 0.0, pltpu.roll(v, 1, 0))
    after = jnp.where(column == count - 1, 0.0, pltpu.roll(v, count - 1, 0))
    return before, after


def dot(a, b):
    return jnp.dot(a, b, preferred_element_type=F32)


def merge_time(source, target):
    cin = source.shape[2]
    step = 64

    def body(n, _):
        at = pl.multiple_of(n * step, step)
        for j in range(3):
            total = source[0, j, pl.ds(at, step), :] + source[1, j, pl.ds(at, step), :]
            target[pl.ds(j * cin + at, step), :] = total
        return 0

    lax.fori_loop(0, cin // step, body, 0)


def merge_space(source, target, step):
    cin, cout = source.shape[3], source.shape[4]

    def body(n, _):
        at = pl.multiple_of(n * step, step)
        for t in range(2):
            tap = {}
            for i in range(3):
                for j in range(3):
                    if t == 0:
                        tap[i, j] = source[0, i, j, pl.ds(at, step), :].astype(F32) + source[
                            1, i, j, pl.ds(at, step), :
                        ].astype(F32)
                    else:
                        tap[i, j] = source[2, i, j, pl.ds(at, step), :].astype(F32)
            for a in range(2):
                for i in range(2):
                    if a == i:
                        lo = i
                        row = [tap[lo, j] + tap[lo + 1, j] for j in range(3)]
                    else:
                        row = [tap[2 * i, j] for j in range(3)]
                    for b in range(2):
                        if b == 0:
                            columns = (row[0] + row[1], row[2])
                        else:
                            columns = (row[0], row[1] + row[2])
                        for j in range(2):
                            target[b, t, i, pl.ds(j * cin + at, step), pl.ds(a * cout, cout)] = columns[
                                j
                            ].astype(BF16)
        return 0

    lax.fori_loop(0, cin // step, body, 0)


def put_cat(target, at, v):
    chans = v.shape[1]
    before, after = shifted(v)
    target[(*at, slice(None), slice(0, chans))] = before.astype(BF16)
    target[(*at, slice(None), slice(chans, 2 * chans))] = v.astype(BF16)
    target[(*at, slice(None), slice(2 * chans, 3 * chans))] = after.astype(BF16)


def load_kernel(own, pair, sem):
    copy = pltpu.make_async_copy(own, pair.at[0], sem)
    copy.start()
    copy.wait()


def pair_kernel(half, other, pair):
    pair[1] = other[...]


def halo_part(source, at, upper, acc, v1, wn, cat):
    cols, c1 = source.shape[2:]
    rows = acc.shape[1] - 3
    size = 2 * cols
    for f in range(2):
        for r in range(2):
            put_cat(cat, (f, r), silu(source[at[f], r].astype(F32)))

    def outer(k, _):
        i = jnp.where(upper, 0, 2)
        both = cat[...].reshape(2 * size, 3 * c1)
        part = dot(both[:size], v1[i])
        total = dot(both, wn[i].reshape(3 * c1, c1))
        m = jnp.where(upper, 0, rows)
        for f in range(2):
            acc[f, pl.ds(m, 2)] += (total[f * size : (f + 1) * size] + part).reshape(2, cols, c1)
        return 0

    def middle(k, _):
        r = jnp.where(upper, 1, 0)
        one = [cat[f, r] for f in range(2)]
        part = dot(one[0], v1[1])
        total = dot(jnp.concatenate(one, axis=0), wn[1].reshape(3 * c1, c1))
        m = jnp.where(upper, 0, rows + 1)
        for f in range(2):
            acc[f, m] += total[f * cols : (f + 1) * cols] + part
        return 0

    lax.fori_loop(0, 1, outer, 0)
    lax.fori_loop(0, 1, middle, 0)


def early_kernel(pair, w1, w2, w3, acc, v1, wn, v2, v3, cat, raw, sems):
    rows, cols, c1 = pair.shape[1:]
    second = lax.axis_index("sect") > 0

    def copy(t, i):
        target = raw.at[i, t] if t < 2 else wn.at[i]
        return pltpu.make_async_copy(w1.at[t, i], target, sems.at[i, t])

    for i in range(3):
        for t in range(3):
            copy(t, i).start()
    for r in range(rows):
        mine, other = pair[0, r].astype(F32), pair[1, r].astype(F32)
        put_cat(cat, (0, r), silu(jnp.where(second, other, mine)))
        put_cat(cat, (1, r), silu(mine))
    merge_space(w3, v3, 16)
    merge_space(w2, v2, 16)
    size = rows * cols
    acc[...] = jnp.zeros(acc.shape, F32)

    def tap(i, _):
        for t in range(3):
            copy(t, i).wait()
        merge_time(raw.at[i], v1.at[i])
        both = cat[...].reshape(2 * size, 3 * c1)
        part = dot(both[:size], v1[i])
        total = dot(both, wn[i].reshape(3 * c1, c1))
        for f in range(2):
            value = (total[f * size : (f + 1) * size] + part).reshape(rows, cols, c1)
            acc[f, pl.ds(2 - i, rows)] += value
        return 0

    lax.fori_loop(0, 3, tap, 0)


def middle_kernel(far, before, v1, wn, acc, cat):
    second = lax.axis_index("sect") > 0
    halo_part(far, (jnp.where(second, 0, 1), 1), second, acc, v1, wn, cat)


def late_kernel(
    pair, far, near, before, v1, wn, b1, v2, b2, v3, b3, out, acc, hcat, mcat, lcat, wide
):
    rows, cols, c1 = pair.shape[1:]
    c2 = b2.shape[0]
    c3 = b3.shape[0]
    second = lax.axis_index("sect") > 0
    tile = lax.axis_index("tile")
    first_tile = tile == 0
    last_tile = tile == lax.axis_size("tile") - 1

    def feature(f, r):
        if r < 2:
            if f == 0:
                return jnp.where(second, far[0, r].astype(F32), near[0, r].astype(F32))
            return jnp.where(second, far[1, r].astype(F32), near[0, r].astype(F32))
        if r < rows + 2:
            mine = pair[0, r - 2].astype(F32)
            if f == 1:
                return mine
            return jnp.where(second, pair[1, r - 2].astype(F32), mine)
        r = r - rows - 2
        if f == 0:
            return jnp.where(second, near[1, r].astype(F32), far[1, r].astype(F32))
        return jnp.where(second, near[0, r].astype(F32), far[1, r].astype(F32))

    mrows = rows + 2
    halo_part(near, (jnp.where(second, 1, 0), 0), jnp.logical_not(second), acc, v1, wn, hcat)
    bias = b1[...].astype(F32)[None, :]
    for f in range(2):
        for m in range(mrows):
            v = acc[f, m] + bias + feature(f, m + 1)
            v = silu(v.astype(BF16).astype(F32))
            if m == 0:
                v = jnp.where(first_tile, 0.0, v)
            if m == mrows - 1:
                v = jnp.where(last_tile, 0.0, v)
            put_cat(mcat, (f, m), v)

    wins = mrows - 1
    bias = b2[...].astype(F32)[None, :]
    for b in range(2):
        lanes = slice(c1, 3 * c1) if b == 0 else slice(0, 2 * c1)
        early = jnp.zeros((wins * cols, 2 * c2), F32)
        now = [early, early]
        for i in range(2):
            lhs = [mcat[f, i : i + wins, :, lanes].reshape(wins * cols, 2 * c1) for f in range(2)]
            early = early + dot(lhs[0], v2[b, 0, i])
            for f in range(2):
                now[f] = now[f] + dot(lhs[f], v2[b, 1, i])
        for f in range(2):
            total = early + now[f]
            for w in range(wins):
                for a in range(2):
                    v = total[w * cols : (w + 1) * cols, a * c2 : (a + 1) * c2] + bias
                    v = silu(v)
                    if w == 0 and a == 0:
                        v = jnp.where(first_tile, 0.0, v)
                    if w == wins - 1 and a == 1:
                        v = jnp.where(last_tile, 0.0, v)
                    before, after = shifted(v)
                    r = 2 * w + a
                    if b == 0:
                        lcat[f, r, :, 0:c2] = before.astype(BF16)
                        lcat[f, r, :, 2 * c2 : 3 * c2] = v.astype(BF16)
                    else:
                        lcat[f, r, :, c2 : 2 * c2] = v.astype(BF16)
                        lcat[f, r, :, 3 * c2 : 4 * c2] = after.astype(BF16)

    lrows = 2 * wins
    wins = lrows - 1
    bias = b3[...].astype(F32)[None, :]
    for q in range(4):
        b = 1 if q % 2 == 0 else 0
        at = (0, c2, c2, 2 * c2)[q]
        lhs = jnp.concatenate(
            [lcat[f, i : i + wins, :, at : at + 2 * c2].reshape(wins * cols, 2 * c2) for f in range(2) for i in range(2)],
            axis=1,
        )
        total = dot(lhs, v3[b].reshape(8 * c2, 2 * c3))
        for o in range(4 * rows):
            a = 1 - o % 2
            w = (o + 1) // 2
            v = total[w * cols : (w + 1) * cols, a * c3 : (a + 1) * c3] + bias
            wide[o, pl.ds(q, cols, stride=4), :] = v
    for o in range(4 * rows):
        out[o] = wide[o].astype(BF16)


def in_vmem(x):
    return pltpu.with_memory_space_constraint(x, pltpu.VMEM)


def per_device(features, conv_first, bias_first, conv_second, bias_second, conv_third, bias_third):
    own = features[0]
    rows, cols, c1 = own.shape
    c2 = conv_second.shape[4]
    c3 = conv_third.shape[4]
    tiles = lax.axis_size("tile")
    swap = [(0, 1), (1, 0)]
    apart = [(i, tiles + i + 1) for i in range(tiles - 1)]
    apart += [(tiles + i + 1, i) for i in range(tiles - 1)]
    vmem = pl.BlockSpec(memory_space=pltpu.VMEM)
    anywhere = pl.BlockSpec(memory_space=pl.ANY)

    other = lax.ppermute(own, "sect", swap)
    pair_shape = pltpu.VMEM((2, rows, cols, c1), BF16)
    half = pl.pallas_call(
        load_kernel,
        out_shape=pair_shape,
        in_specs=[anywhere],
        out_specs=vmem,
        scratch_shapes=[pltpu.SemaphoreType.DMA],
        cost_estimate=pl.CostEstimate(flops=6_000_000_000, bytes_accessed=1024, transcendentals=0),
        compiler_params=pltpu.CompilerParams(vmem_limit_bytes=1 << 20),
    )(pltpu.with_memory_space_constraint(own, pltpu.HBM))
    pair = pl.pallas_call(
        pair_kernel,
        out_shape=pair_shape,
        in_specs=[vmem] * 2,
        out_specs=vmem,
        input_output_aliases={0: 0},
        cost_estimate=pl.CostEstimate(flops=6_000_000_000, bytes_accessed=1024, transcendentals=0),
        compiler_params=pltpu.CompilerParams(vmem_limit_bytes=1 << 20),
    )(in_vmem(half), in_vmem(other))
    if rows == 2:
        edge = pair
    else:
        edge = jnp.where(lax.axis_index("sect") == 0, pair[:, rows - 2 :], pair[:, :2])
    far = lax.ppermute(edge, ("sect", "tile"), apart)
    near = lax.ppermute(far, "sect", swap)
    acc, v1, wn, v2, v3 = pl.pallas_call(
        early_kernel,
        out_shape=[
            pltpu.VMEM((2, rows + 3, cols, c1), F32),
            pltpu.VMEM((3, 3 * c1, c1), BF16),
            pltpu.VMEM((3, 3, c1, c1), BF16),
            pltpu.VMEM((2, 2, 2, 2 * c1, 2 * c2), BF16),
            pltpu.VMEM((2, 2, 2, 2 * c2, 2 * c3), BF16),
        ],
        in_specs=[vmem, anywhere, vmem, vmem],
        out_specs=[vmem] * 5,
        scratch_shapes=[
            pltpu.VMEM((2, rows, cols, 3 * c1), BF16),
            pltpu.VMEM((3, 2, 3, c1, c1), BF16),
            pltpu.SemaphoreType.DMA((3, 3)),
        ],
        cost_estimate=pl.CostEstimate(flops=6_000_000_000, bytes_accessed=1024, transcendentals=0),
        compiler_params=pltpu.CompilerParams(vmem_limit_bytes=16 << 20),
    )(
        in_vmem(pair),
        pltpu.with_memory_space_constraint(conv_first, pltpu.HBM),
        in_vmem(conv_second),
        in_vmem(conv_third),
    )
    acc_shape = pltpu.VMEM((2, rows + 3, cols, c1), F32)
    acc = pl.pallas_call(
        middle_kernel,
        out_shape=acc_shape,
        in_specs=[vmem] * 4,
        out_specs=vmem,
        input_output_aliases={1: 0},
        scratch_shapes=[pltpu.VMEM((2, 2, cols, 3 * c1), BF16)],
        cost_estimate=pl.CostEstimate(flops=2_000_000_000, bytes_accessed=1024, transcendentals=0),
        compiler_params=pltpu.CompilerParams(vmem_limit_bytes=8 << 20),
    )(in_vmem(far), in_vmem(acc), in_vmem(v1), in_vmem(wn))
    out, _ = pl.pallas_call(
        late_kernel,
        out_shape=[jax.ShapeDtypeStruct((4 * rows, 4 * cols, c3), BF16), acc_shape],
        in_specs=[vmem] * 11,
        out_specs=[vmem] * 2,
        input_output_aliases={3: 1},
        scratch_shapes=[
            pltpu.VMEM((2, 2, cols, 3 * c1), BF16),
            pltpu.VMEM((2, rows + 2, cols, 3 * c1), BF16),
            pltpu.VMEM((2, 2 * rows + 2, cols, 4 * c2), BF16),
            pltpu.VMEM((4 * rows, 4 * cols, c3), F32),
        ],
        cost_estimate=pl.CostEstimate(flops=8_000_000_000, bytes_accessed=1024, transcendentals=0),
        compiler_params=pltpu.CompilerParams(vmem_limit_bytes=14 << 20),
    )(
        in_vmem(pair),
        in_vmem(far),
        in_vmem(near),
        in_vmem(acc),
        in_vmem(v1),
        in_vmem(wn),
        bias_first,
        in_vmem(v2),
        bias_second,
        in_vmem(v3),
        bias_third,
    )
    return out[None]


def solution(mesh):
    return jax.shard_map(
        per_device,
        mesh=mesh,
        in_specs=(P(("groups", "sect"), "tile", None, None), P(), P(), P(), P(), P(), P()),
        out_specs=P(("groups", "sect"), "tile", None, None),
        check_vma=False,
    )
```

```python
import jax
import jax.numpy as jnp
from jax import lax
from jax.experimental import pallas as pl
from jax.experimental.pallas import tpu as pltpu
from jax.sharding import PartitionSpec as P

F32 = jnp.float32
BF16 = jnp.bfloat16


def silu(v):
    half = 0.5 * v
    return half + half * jnp.tanh(half)


def shifted(v):
    count = v.shape[0]
    column = lax.broadcasted_iota(jnp.int32, v.shape, 0)
    before = jnp.where(column == 0, 0.0, pltpu.roll(v, 1, 0))
    after = jnp.where(column == count - 1, 0.0, pltpu.roll(v, count - 1, 0))
    return before, after


def dot(a, b):
    return jnp.dot(a, b, preferred_element_type=F32)


def merge_time(source, target):
    cin = source.shape[2]
    step = 64

    def body(n, _):
        at = pl.multiple_of(n * step, step)
        for j in range(3):
            total = source[0, j, pl.ds(at, step), :] + source[1, j, pl.ds(at, step), :]
            target[pl.ds(j * cin + at, step), :] = total
        return 0

    lax.fori_loop(0, cin // step, body, 0)


def merge_space(source, target, step):
    cin, cout = source.shape[3], source.shape[4]

    def body(n, _):
        at = pl.multiple_of(n * step, step)
        for t in range(2):
            tap = {}
            for i in range(3):
                for j in range(3):
                    if t == 0:
                        tap[i, j] = source[0, i, j, pl.ds(at, step), :].astype(F32) + source[
                            1, i, j, pl.ds(at, step), :
                        ].astype(F32)
                    else:
                        tap[i, j] = source[2, i, j, pl.ds(at, step), :].astype(F32)
            for a in range(2):
                for i in range(2):
                    if a == i:
                        lo = i
                        row = [tap[lo, j] + tap[lo + 1, j] for j in range(3)]
                    else:
                        row = [tap[2 * i, j] for j in range(3)]
                    for b in range(2):
                        if b == 0:
                            columns = (row[0] + row[1], row[2])
                        else:
                            columns = (row[0], row[1] + row[2])
                        for j in range(2):
                            target[b, t, i, pl.ds(j * cin + at, step), pl.ds(a * cout, cout)] = columns[
                                j
                            ].astype(BF16)
        return 0

    lax.fori_loop(0, cin // step, body, 0)


def put_cat(target, at, v):
    chans = v.shape[1]
    before, after = shifted(v)
    target[(*at, slice(None), slice(0, chans))] = before.astype(BF16)
    target[(*at, slice(None), slice(chans, 2 * chans))] = v.astype(BF16)
    target[(*at, slice(None), slice(2 * chans, 3 * chans))] = after.astype(BF16)


def load_kernel(own, pair, sem):
    copy = pltpu.make_async_copy(own, pair.at[0], sem)
    copy.start()
    copy.wait()


def pair_kernel(half, other, pair):
    pair[1] = other[...]


def halo_part(source, at, upper, acc, v1, wn, cat):
    cols, c1 = source.shape[2:]
    rows = acc.shape[1] - 3
    size = 2 * cols
    for f in range(2):
        for r in range(2):
            put_cat(cat, (f, r), silu(source[at[f], r].astype(F32)))

    def outer(k, _):
        i = jnp.where(upper, 0, 2)
        both = cat[...].reshape(2 * size, 3 * c1)
        part = dot(both[:size], v1[i])
        total = dot(both, wn[i].reshape(3 * c1, c1))
        m = jnp.where(upper, 0, rows)
        for f in range(2):
            acc[f, pl.ds(m, 2)] += (total[f * size : (f + 1) * size] + part).reshape(2, cols, c1)
        return 0

    def middle(k, _):
        r = jnp.where(upper, 1, 0)
        one = [cat[f, r] for f in range(2)]
        part = dot(one[0], v1[1])
        total = dot(jnp.concatenate(one, axis=0), wn[1].reshape(3 * c1, c1))
        m = jnp.where(upper, 0, rows + 1)
        for f in range(2):
            acc[f, m] += total[f * cols : (f + 1) * cols] + part
        return 0

    lax.fori_loop(0, 1, outer, 0)
    lax.fori_loop(0, 1, middle, 0)


def early_kernel(pair, w1, w2, w3, acc, v1, wn, v2, v3, cat, raw, sems):
    rows, cols, c1 = pair.shape[1:]
    second = lax.axis_index("sect") > 0

    def copy(t, i):
        target = raw.at[i, t] if t < 2 else wn.at[i]
        return pltpu.make_async_copy(w1.at[t, i], target, sems.at[i, t])

    for i in range(3):
        for t in range(3):
            copy(t, i).start()
    for r in range(rows):
        mine, other = pair[0, r].astype(F32), pair[1, r].astype(F32)
        put_cat(cat, (0, r), silu(jnp.where(second, other, mine)))
        put_cat(cat, (1, r), silu(mine))
    merge_space(w3, v3, 16)
    merge_space(w2, v2, 16)
    size = rows * cols
    acc[...] = jnp.zeros(acc.shape, F32)

    def tap(i, _):
        for t in range(3):
            copy(t, i).wait()
        merge_time(raw.at[i], v1.at[i])
        both = cat[...].reshape(2 * size, 3 * c1)
        part = dot(both[:size], v1[i])
        total = dot(both, wn[i].reshape(3 * c1, c1))
        for f in range(2):
            value = (total[f * size : (f + 1) * size] + part).reshape(rows, cols, c1)
            acc[f, pl.ds(2 - i, rows)] += value
        return 0

    lax.fori_loop(0, 3, tap, 0)


def middle_kernel(far, before, v1, wn, acc, cat):
    second = lax.axis_index("sect") > 0
    halo_part(far, (jnp.where(second, 0, 1), 1), second, acc, v1, wn, cat)


def late_kernel(
    pair, far, near, before, v1, wn, b1, v2, b2, v3, b3, out, acc, hcat, mcat, lcat, wide, narrow, sems
):
    rows, cols, c1 = pair.shape[1:]
    c2 = b2.shape[0]
    c3 = b3.shape[0]
    second = lax.axis_index("sect") > 0
    tile = lax.axis_index("tile")
    first_tile = tile == 0
    last_tile = tile == lax.axis_size("tile") - 1

    def feature(f, r):
        if r < 2:
            if f == 0:
                return jnp.where(second, far[0, r].astype(F32), near[0, r].astype(F32))
            return jnp.where(second, far[1, r].astype(F32), near[0, r].astype(F32))
        if r < rows + 2:
            mine = pair[0, r - 2].astype(F32)
            if f == 1:
                return mine
            return jnp.where(second, pair[1, r - 2].astype(F32), mine)
        r = r - rows - 2
        if f == 0:
            return jnp.where(second, near[1, r].astype(F32), far[1, r].astype(F32))
        return jnp.where(second, near[0, r].astype(F32), far[1, r].astype(F32))

    mrows = rows + 2
    halo_part(near, (jnp.where(second, 1, 0), 0), jnp.logical_not(second), acc, v1, wn, hcat)
    bias = b1[...].astype(F32)[None, :]
    for f in range(2):
        for m in range(mrows):
            v = acc[f, m] + bias + feature(f, m + 1)
            v = silu(v.astype(BF16).astype(F32))
            if m == 0:
                v = jnp.where(first_tile, 0.0, v)
            if m == mrows - 1:
                v = jnp.where(last_tile, 0.0, v)
            put_cat(mcat, (f, m), v)

    wins = mrows - 1
    bias = b2[...].astype(F32)[None, :]
    for b in range(2):
        lanes = slice(c1, 3 * c1) if b == 0 else slice(0, 2 * c1)
        early = jnp.zeros((wins * cols, 2 * c2), F32)
        now = [early, early]
        for i in range(2):
            lhs = [mcat[f, i : i + wins, :, lanes].reshape(wins * cols, 2 * c1) for f in range(2)]
            early = early + dot(lhs[0], v2[b, 0, i])
            for f in range(2):
                now[f] = now[f] + dot(lhs[f], v2[b, 1, i])
        for f in range(2):
            total = early + now[f]
            for w in range(wins):
                for a in range(2):
                    v = total[w * cols : (w + 1) * cols, a * c2 : (a + 1) * c2] + bias
                    v = silu(v)
                    if w == 0 and a == 0:
                        v = jnp.where(first_tile, 0.0, v)
                    if w == wins - 1 and a == 1:
                        v = jnp.where(last_tile, 0.0, v)
                    before, after = shifted(v)
                    r = 2 * w + a
                    if b == 0:
                        lcat[f, r, :, 0:c2] = before.astype(BF16)
                        lcat[f, r, :, 2 * c2 : 3 * c2] = v.astype(BF16)
                    else:
                        lcat[f, r, :, c2 : 2 * c2] = v.astype(BF16)
                        lcat[f, r, :, 3 * c2 : 4 * c2] = after.astype(BF16)

    lrows = 2 * wins
    wins = lrows - 1
    bias = b3[...].astype(F32)[None, :]
    for q in range(4):
        b = 1 if q % 2 == 0 else 0
        at = (0, c2, c2, 2 * c2)[q]
        lhs = jnp.concatenate(
            [lcat[f, i : i + wins, :, at : at + 2 * c2].reshape(wins * cols, 2 * c2) for f in range(2) for i in range(2)],
            axis=1,
        )
        total = dot(lhs, v3[b].reshape(8 * c2, 2 * c3))
        for o in range(4 * rows):
            a = 1 - o % 2
            w = (o + 1) // 2
            v = total[w * cols : (w + 1) * cols, a * c3 : (a + 1) * c3] + bias
            wide[o, pl.ds(q, cols, stride=4), :] = v
    copies = [pltpu.make_async_copy(narrow.at[o], out.at[o], sems.at[o]) for o in range(4 * rows)]
    for o in range(4 * rows):
        narrow[o] = wide[o].astype(BF16)
        copies[o].start()
    for copy in copies:
        copy.wait()


def in_vmem(x):
    return pltpu.with_memory_space_constraint(x, pltpu.VMEM)


def per_device(features, conv_first, bias_first, conv_second, bias_second, conv_third, bias_third):
    own = features[0]
    rows, cols, c1 = own.shape
    c2 = conv_second.shape[4]
    c3 = conv_third.shape[4]
    tiles = lax.axis_size("tile")
    swap = [(0, 1), (1, 0)]
    apart = [(i, tiles + i + 1) for i in range(tiles - 1)]
    apart += [(tiles + i + 1, i) for i in range(tiles - 1)]
    vmem = pl.BlockSpec(memory_space=pltpu.VMEM)
    anywhere = pl.BlockSpec(memory_space=pl.ANY)

    other = lax.ppermute(own, "sect", swap)
    pair_shape = pltpu.VMEM((2, rows, cols, c1), BF16)
    half = pl.pallas_call(
        load_kernel,
        out_shape=pair_shape,
        in_specs=[anywhere],
        out_specs=vmem,
        scratch_shapes=[pltpu.SemaphoreType.DMA],
        cost_estimate=pl.CostEstimate(flops=6_000_000_000, bytes_accessed=1024, transcendentals=0),
        compiler_params=pltpu.CompilerParams(vmem_limit_bytes=1 << 20),
    )(pltpu.with_memory_space_constraint(own, pltpu.HBM))
    pair = pl.pallas_call(
        pair_kernel,
        out_shape=pair_shape,
        in_specs=[vmem] * 2,
        out_specs=vmem,
        input_output_aliases={0: 0},
        cost_estimate=pl.CostEstimate(flops=6_000_000_000, bytes_accessed=1024, transcendentals=0),
        compiler_params=pltpu.CompilerParams(vmem_limit_bytes=1 << 20),
    )(in_vmem(half), in_vmem(other))
    if rows == 2:
        edge = pair
    else:
        edge = jnp.where(lax.axis_index("sect") == 0, pair[:, rows - 2 :], pair[:, :2])
    far = lax.ppermute(edge, ("sect", "tile"), apart)
    near = lax.ppermute(far, "sect", swap)
    acc, v1, wn, v2, v3 = pl.pallas_call(
        early_kernel,
        out_shape=[
            pltpu.VMEM((2, rows + 3, cols, c1), F32),
            pltpu.VMEM((3, 3 * c1, c1), BF16),
            pltpu.VMEM((3, 3, c1, c1), BF16),
            pltpu.VMEM((2, 2, 2, 2 * c1, 2 * c2), BF16),
            pltpu.VMEM((2, 2, 2, 2 * c2, 2 * c3), BF16),
        ],
        in_specs=[vmem, anywhere, vmem, vmem],
        out_specs=[vmem] * 5,
        scratch_shapes=[
            pltpu.VMEM((2, rows, cols, 3 * c1), BF16),
            pltpu.VMEM((3, 2, 3, c1, c1), BF16),
            pltpu.SemaphoreType.DMA((3, 3)),
        ],
        cost_estimate=pl.CostEstimate(flops=6_000_000_000, bytes_accessed=1024, transcendentals=0),
        compiler_params=pltpu.CompilerParams(vmem_limit_bytes=16 << 20),
    )(
        in_vmem(pair),
        pltpu.with_memory_space_constraint(conv_first, pltpu.HBM),
        in_vmem(conv_second),
        in_vmem(conv_third),
    )
    acc_shape = pltpu.VMEM((2, rows + 3, cols, c1), F32)
    acc = pl.pallas_call(
        middle_kernel,
        out_shape=acc_shape,
        in_specs=[vmem] * 4,
        out_specs=vmem,
        input_output_aliases={1: 0},
        scratch_shapes=[pltpu.VMEM((2, 2, cols, 3 * c1), BF16)],
        cost_estimate=pl.CostEstimate(flops=2_000_000_000, bytes_accessed=1024, transcendentals=0),
        compiler_params=pltpu.CompilerParams(vmem_limit_bytes=8 << 20),
    )(in_vmem(far), in_vmem(acc), in_vmem(v1), in_vmem(wn))
    out, _ = pl.pallas_call(
        late_kernel,
        out_shape=[jax.ShapeDtypeStruct((4 * rows, 4 * cols, c3), BF16), acc_shape],
        in_specs=[vmem] * 11,
        out_specs=[anywhere, vmem],
        input_output_aliases={3: 1},
        scratch_shapes=[
            pltpu.VMEM((2, 2, cols, 3 * c1), BF16),
            pltpu.VMEM((2, rows + 2, cols, 3 * c1), BF16),
            pltpu.VMEM((2, 2 * rows + 2, cols, 4 * c2), BF16),
            pltpu.VMEM((4 * rows, 4 * cols, c3), F32),
            pltpu.VMEM((4 * rows, 4 * cols, c3), BF16),
            pltpu.SemaphoreType.DMA((4 * rows,)),
        ],
        cost_estimate=pl.CostEstimate(flops=8_000_000_000, bytes_accessed=1024, transcendentals=0),
        compiler_params=pltpu.CompilerParams(vmem_limit_bytes=14 << 20),
    )(
        in_vmem(pair),
        in_vmem(far),
        in_vmem(near),
        in_vmem(acc),
        in_vmem(v1),
        in_vmem(wn),
        bias_first,
        in_vmem(v2),
        bias_second,
        in_vmem(v3),
        bias_third,
    )
    return out[None]


def solution(mesh):
    return jax.shard_map(
        per_device,
        mesh=mesh,
        in_specs=(P(("groups", "sect"), "tile", None, None), P(), P(), P(), P(), P(), P()),
        out_specs=P(("groups", "sect"), "tile", None, None),
        check_vma=False,
    )
```

```python
import jax
import jax.numpy as jnp
from jax import lax
from jax.experimental import pallas as pl
from jax.experimental.pallas import tpu as pltpu
from jax.sharding import PartitionSpec as P

F32 = jnp.float32
BF16 = jnp.bfloat16


def silu(v):
    half = 0.5 * v
    return half + half * jnp.tanh(half)


def shifted(v):
    count = v.shape[0]
    column = lax.broadcasted_iota(jnp.int32, v.shape, 0)
    before = jnp.where(column == 0, 0.0, pltpu.roll(v, 1, 0))
    after = jnp.where(column == count - 1, 0.0, pltpu.roll(v, count - 1, 0))
    return before, after


def dot(a, b):
    return jnp.dot(a, b, preferred_element_type=F32)


def merge_time(source, target):
    cin = source.shape[2]
    step = 64

    def body(n, _):
        at = pl.multiple_of(n * step, step)
        for j in range(3):
            total = source[0, j, pl.ds(at, step), :] + source[1, j, pl.ds(at, step), :]
            target[pl.ds(j * cin + at, step), :] = total
        return 0

    lax.fori_loop(0, cin // step, body, 0)


def merge_space(source, target, step):
    cin, cout = source.shape[3], source.shape[4]

    def body(n, _):
        at = pl.multiple_of(n * step, step)
        for t in range(2):
            tap = {}
            for i in range(3):
                for j in range(3):
                    if t == 0:
                        tap[i, j] = source[0, i, j, pl.ds(at, step), :].astype(F32) + source[
                            1, i, j, pl.ds(at, step), :
                        ].astype(F32)
                    else:
                        tap[i, j] = source[2, i, j, pl.ds(at, step), :].astype(F32)
            for a in range(2):
                for i in range(2):
                    if a == i:
                        lo = i
                        row = [tap[lo, j] + tap[lo + 1, j] for j in range(3)]
                    else:
                        row = [tap[2 * i, j] for j in range(3)]
                    for b in range(2):
                        if b == 0:
                            columns = (row[0] + row[1], row[2])
                        else:
                            columns = (row[0], row[1] + row[2])
                        for j in range(2):
                            target[b, t, i, pl.ds(j * cin + at, step), pl.ds(a * cout, cout)] = columns[
                                j
                            ].astype(BF16)
        return 0

    lax.fori_loop(0, cin // step, body, 0)


def put_cat(target, at, v):
    chans = v.shape[1]
    before, after = shifted(v)
    target[(*at, slice(None), slice(0, chans))] = before.astype(BF16)
    target[(*at, slice(None), slice(chans, 2 * chans))] = v.astype(BF16)
    target[(*at, slice(None), slice(2 * chans, 3 * chans))] = after.astype(BF16)


def load_kernel(own, pair, sem):
    copy = pltpu.make_async_copy(own, pair.at[0], sem)
    copy.start()
    copy.wait()


def pair_kernel(half, other, pair):
    pair[1] = other[...]


def far_above():
    return (lax.axis_index("sect") + lax.axis_index("tile")) % 2 == 1


def halo_part(source, at, upper, acc, v1, wn, cat):
    cols, c1 = source.shape[2:]
    rows = acc.shape[1] - 3
    size = 2 * cols
    for f in range(2):
        for r in range(2):
            put_cat(cat, (f, r), silu(source[at[f], r].astype(F32)))

    def outer(k, _):
        i = jnp.where(upper, 0, 2)
        both = cat[...].reshape(2 * size, 3 * c1)
        part = dot(both[:size], v1[i])
        total = dot(both, wn[i].reshape(3 * c1, c1))
        m = jnp.where(upper, 0, rows)
        for f in range(2):
            acc[f, pl.ds(m, 2)] += (total[f * size : (f + 1) * size] + part).reshape(2, cols, c1)
        return 0

    def middle(k, _):
        r = jnp.where(upper, 1, 0)
        one = [cat[f, r] for f in range(2)]
        part = dot(one[0], v1[1])
        total = dot(jnp.concatenate(one, axis=0), wn[1].reshape(3 * c1, c1))
        m = jnp.where(upper, 0, rows + 1)
        for f in range(2):
            acc[f, m] += total[f * cols : (f + 1) * cols] + part
        return 0

    lax.fori_loop(0, 1, outer, 0)
    lax.fori_loop(0, 1, middle, 0)


def early_kernel(pair, w1, w2, w3, acc, v1, wn, v2, v3, cat, raw, sems):
    rows, cols, c1 = pair.shape[1:]
    second = lax.axis_index("sect") > 0

    def copy(t, i):
        target = raw.at[i, t] if t < 2 else wn.at[i]
        return pltpu.make_async_copy(w1.at[t, i], target, sems.at[i, t])

    for i in range(3):
        for t in range(3):
            copy(t, i).start()
    for r in range(rows):
        mine, other = pair[0, r].astype(F32), pair[1, r].astype(F32)
        put_cat(cat, (0, r), silu(jnp.where(second, other, mine)))
        put_cat(cat, (1, r), silu(mine))
    merge_space(w3, v3, 16)
    merge_space(w2, v2, 16)
    size = rows * cols
    acc[...] = jnp.zeros(acc.shape, F32)

    def tap(i, _):
        for t in range(3):
            copy(t, i).wait()
        merge_time(raw.at[i], v1.at[i])
        both = cat[...].reshape(2 * size, 3 * c1)
        part = dot(both[:size], v1[i])
        total = dot(both, wn[i].reshape(3 * c1, c1))
        for f in range(2):
            value = (total[f * size : (f + 1) * size] + part).reshape(rows, cols, c1)
            acc[f, pl.ds(2 - i, rows)] += value
        return 0

    lax.fori_loop(0, 3, tap, 0)


def middle_kernel(far, before, v1, wn, acc, cat):
    second = lax.axis_index("sect") > 0
    halo_part(far, (jnp.where(second, 1, 0), 0), far_above(), acc, v1, wn, cat)


def late_kernel(
    pair, far, near, before, v1, wn, b1, v2, b2, v3, b3, out, acc, hcat, mcat, lcat, wide, narrow, sems
):
    rows, cols, c1 = pair.shape[1:]
    c2 = b2.shape[0]
    c3 = b3.shape[0]
    second = lax.axis_index("sect") > 0
    tile = lax.axis_index("tile")
    first_tile = tile == 0
    last_tile = tile == lax.axis_size("tile") - 1

    def feature(f, r):
        if 2 <= r < rows + 2:
            mine = pair[0, r - 2].astype(F32)
            if f == 1:
                return mine
            return jnp.where(second, pair[1, r - 2].astype(F32), mine)
        above = r < 2
        r = r if above else r - rows - 2
        if f == 1:
            own, other = far[0, r].astype(F32), near[1, r].astype(F32)
        else:
            own = jnp.where(second, far[1, r].astype(F32), far[0, r].astype(F32))
            other = jnp.where(second, near[0, r].astype(F32), near[1, r].astype(F32))
        upper = far_above()
        return jnp.where(upper if above else jnp.logical_not(upper), own, other)

    mrows = rows + 2
    halo_part(near, (jnp.where(second, 0, 1), 1), jnp.logical_not(far_above()), acc, v1, wn, hcat)
    bias = b1[...].astype(F32)[None, :]
    for f in range(2):
        for m in range(mrows):
            v = acc[f, m] + bias + feature(f, m + 1)
            v = silu(v.astype(BF16).astype(F32))
            if m == 0:
                v = jnp.where(first_tile, 0.0, v)
            if m == mrows - 1:
                v = jnp.where(last_tile, 0.0, v)
            put_cat(mcat, (f, m), v)

    wins = mrows - 1
    bias = b2[...].astype(F32)[None, :]
    for b in range(2):
        lanes = slice(c1, 3 * c1) if b == 0 else slice(0, 2 * c1)
        early = jnp.zeros((wins * cols, 2 * c2), F32)
        now = [early, early]
        for i in range(2):
            lhs = [mcat[f, i : i + wins, :, lanes].reshape(wins * cols, 2 * c1) for f in range(2)]
            early = early + dot(lhs[0], v2[b, 0, i])
            for f in range(2):
                now[f] = now[f] + dot(lhs[f], v2[b, 1, i])
        for f in range(2):
            total = early + now[f]
            for w in range(wins):
                for a in range(2):
                    v = total[w * cols : (w + 1) * cols, a * c2 : (a + 1) * c2] + bias
                    v = silu(v)
                    if w == 0 and a == 0:
                        v = jnp.where(first_tile, 0.0, v)
                    if w == wins - 1 and a == 1:
                        v = jnp.where(last_tile, 0.0, v)
                    before, after = shifted(v)
                    r = 2 * w + a
                    if b == 0:
                        lcat[f, r, :, 0:c2] = before.astype(BF16)
                        lcat[f, r, :, 2 * c2 : 3 * c2] = v.astype(BF16)
                    else:
                        lcat[f, r, :, c2 : 2 * c2] = v.astype(BF16)
                        lcat[f, r, :, 3 * c2 : 4 * c2] = after.astype(BF16)

    lrows = 2 * wins
    wins = lrows - 1
    bias = b3[...].astype(F32)[None, :]
    for q in range(4):
        b = 1 if q % 2 == 0 else 0
        at = (0, c2, c2, 2 * c2)[q]
        lhs = jnp.concatenate(
            [lcat[f, i : i + wins, :, at : at + 2 * c2].reshape(wins * cols, 2 * c2) for f in range(2) for i in range(2)],
            axis=1,
        )
        total = dot(lhs, v3[b].reshape(8 * c2, 2 * c3))
        for o in range(4 * rows):
            a = 1 - o % 2
            w = (o + 1) // 2
            v = total[w * cols : (w + 1) * cols, a * c3 : (a + 1) * c3] + bias
            wide[o, pl.ds(q, cols, stride=4), :] = v
    copies = [pltpu.make_async_copy(narrow.at[o], out.at[o], sems.at[o]) for o in range(4 * rows)]
    for o in range(4 * rows):
        narrow[o] = wide[o].astype(BF16)
        copies[o].start()
    for copy in copies:
        copy.wait()


def in_vmem(x):
    return pltpu.with_memory_space_constraint(x, pltpu.VMEM)


def per_device(features, conv_first, bias_first, conv_second, bias_second, conv_third, bias_third):
    own = features[0]
    rows, cols, c1 = own.shape
    c2 = conv_second.shape[4]
    c3 = conv_third.shape[4]
    tiles = lax.axis_size("tile")
    swap = [(0, 1), (1, 0)]
    apart = []
    for i in range(tiles - 1):
        core = tiles * (i % 2)
        apart += [(core + i, core + i + 1), (core + i + 1, core + i)]
    vmem = pl.BlockSpec(memory_space=pltpu.VMEM)
    anywhere = pl.BlockSpec(memory_space=pl.ANY)

    other = lax.ppermute(own, "sect", swap)
    pair_shape = pltpu.VMEM((2, rows, cols, c1), BF16)
    half = pl.pallas_call(
        load_kernel,
        out_shape=pair_shape,
        in_specs=[anywhere],
        out_specs=vmem,
        scratch_shapes=[pltpu.SemaphoreType.DMA],
        cost_estimate=pl.CostEstimate(flops=6_000_000_000, bytes_accessed=1024, transcendentals=0),
        compiler_params=pltpu.CompilerParams(vmem_limit_bytes=1 << 20),
    )(pltpu.with_memory_space_constraint(own, pltpu.HBM))
    pair = pl.pallas_call(
        pair_kernel,
        out_shape=pair_shape,
        in_specs=[vmem] * 2,
        out_specs=vmem,
        input_output_aliases={0: 0},
        cost_estimate=pl.CostEstimate(flops=6_000_000_000, bytes_accessed=1024, transcendentals=0),
        compiler_params=pltpu.CompilerParams(vmem_limit_bytes=1 << 20),
    )(in_vmem(half), in_vmem(other))
    if rows == 2:
        edge = pair
    else:
        edge = jnp.where(far_above(), pair[:, :2], pair[:, rows - 2 :])
    far = lax.ppermute(edge, ("sect", "tile"), apart)
    near = lax.ppermute(far, "sect", swap)
    acc, v1, wn, v2, v3 = pl.pallas_call(
        early_kernel,
        out_shape=[
            pltpu.VMEM((2, rows + 3, cols, c1), F32),
            pltpu.VMEM((3, 3 * c1, c1), BF16),
            pltpu.VMEM((3, 3, c1, c1), BF16),
            pltpu.VMEM((2, 2, 2, 2 * c1, 2 * c2), BF16),
            pltpu.VMEM((2, 2, 2, 2 * c2, 2 * c3), BF16),
        ],
        in_specs=[vmem, anywhere, vmem, vmem],
        out_specs=[vmem] * 5,
        scratch_shapes=[
            pltpu.VMEM((2, rows, cols, 3 * c1), BF16),
            pltpu.VMEM((3, 2, 3, c1, c1), BF16),
            pltpu.SemaphoreType.DMA((3, 3)),
        ],
        cost_estimate=pl.CostEstimate(flops=6_000_000_000, bytes_accessed=1024, transcendentals=0),
        compiler_params=pltpu.CompilerParams(vmem_limit_bytes=16 << 20),
    )(
        in_vmem(pair),
        pltpu.with_memory_space_constraint(conv_first, pltpu.HBM),
        in_vmem(conv_second),
        in_vmem(conv_third),
    )
    acc_shape = pltpu.VMEM((2, rows + 3, cols, c1), F32)
    acc = pl.pallas_call(
        middle_kernel,
        out_shape=acc_shape,
        in_specs=[vmem] * 4,
        out_specs=vmem,
        input_output_aliases={1: 0},
        scratch_shapes=[pltpu.VMEM((2, 2, cols, 3 * c1), BF16)],
        cost_estimate=pl.CostEstimate(flops=2_000_000_000, bytes_accessed=1024, transcendentals=0),
        compiler_params=pltpu.CompilerParams(vmem_limit_bytes=8 << 20),
    )(in_vmem(far), in_vmem(acc), in_vmem(v1), in_vmem(wn))
    out, _ = pl.pallas_call(
        late_kernel,
        out_shape=[jax.ShapeDtypeStruct((4 * rows, 4 * cols, c3), BF16), acc_shape],
        in_specs=[vmem] * 11,
        out_specs=[anywhere, vmem],
        input_output_aliases={3: 1},
        scratch_shapes=[
            pltpu.VMEM((2, 2, cols, 3 * c1), BF16),
            pltpu.VMEM((2, rows + 2, cols, 3 * c1), BF16),
            pltpu.VMEM((2, 2 * rows + 2, cols, 4 * c2), BF16),
            pltpu.VMEM((4 * rows, 4 * cols, c3), F32),
            pltpu.VMEM((4 * rows, 4 * cols, c3), BF16),
            pltpu.SemaphoreType.DMA((4 * rows,)),
        ],
        cost_estimate=pl.CostEstimate(flops=8_000_000_000, bytes_accessed=1024, transcendentals=0),
        compiler_params=pltpu.CompilerParams(vmem_limit_bytes=14 << 20),
    )(
        in_vmem(pair),
        in_vmem(far),
        in_vmem(near),
        in_vmem(acc),
        in_vmem(v1),
        in_vmem(wn),
        bias_first,
        in_vmem(v2),
        bias_second,
        in_vmem(v3),
        bias_third,
    )
    return out[None]


def solution(mesh):
    return jax.shard_map(
        per_device,
        mesh=mesh,
        in_specs=(P(("groups", "sect"), "tile", None, None), P(), P(), P(), P(), P(), P()),
        out_specs=P(("groups", "sect"), "tile", None, None),
        check_vma=False,
    )
```

```python
import jax
import jax.numpy as jnp
from jax import lax
from jax.experimental import pallas as pl
from jax.experimental.pallas import tpu as pltpu
from jax.sharding import PartitionSpec as P

F32 = jnp.float32
BF16 = jnp.bfloat16


def silu(v):
    half = 0.5 * v
    return half + half * jnp.tanh(half)


def shifted(v):
    count = v.shape[0]
    column = lax.broadcasted_iota(jnp.int32, v.shape, 0)
    before = jnp.where(column == 0, 0.0, pltpu.roll(v, 1, 0))
    after = jnp.where(column == count - 1, 0.0, pltpu.roll(v, count - 1, 0))
    return before, after


def dot(a, b):
    return jnp.dot(a, b, preferred_element_type=F32)


def merge_time(source, target):
    cin = source.shape[2]
    step = 64

    def body(n, _):
        at = pl.multiple_of(n * step, step)
        for j in range(3):
            total = source[0, j, pl.ds(at, step), :] + source[1, j, pl.ds(at, step), :]
            target[pl.ds(j * cin + at, step), :] = total
        return 0

    lax.fori_loop(0, cin // step, body, 0)


def merge_space(source, target, step):
    cin, cout = source.shape[3], source.shape[4]

    def body(n, _):
        at = pl.multiple_of(n * step, step)
        for t in range(2):
            tap = {}
            for i in range(3):
                for j in range(3):
                    if t == 0:
                        tap[i, j] = source[0, i, j, pl.ds(at, step), :].astype(F32) + source[
                            1, i, j, pl.ds(at, step), :
                        ].astype(F32)
                    else:
                        tap[i, j] = source[2, i, j, pl.ds(at, step), :].astype(F32)
            for a in range(2):
                for i in range(2):
                    if a == i:
                        lo = i
                        row = [tap[lo, j] + tap[lo + 1, j] for j in range(3)]
                    else:
                        row = [tap[2 * i, j] for j in range(3)]
                    for b in range(2):
                        if b == 0:
                            columns = (row[0] + row[1], row[2])
                        else:
                            columns = (row[0], row[1] + row[2])
                        for j in range(2):
                            target[b, t, i, pl.ds(j * cin + at, step), pl.ds(a * cout, cout)] = columns[
                                j
                            ].astype(BF16)
        return 0

    lax.fori_loop(0, cin // step, body, 0)


def put_cat(target, at, v):
    chans = v.shape[1]
    before, after = shifted(v)
    target[(*at, slice(None), slice(0, chans))] = before.astype(BF16)
    target[(*at, slice(None), slice(chans, 2 * chans))] = v.astype(BF16)
    target[(*at, slice(None), slice(2 * chans, 3 * chans))] = after.astype(BF16)


def load_kernel(own, pair, sem):
    copy = pltpu.make_async_copy(own, pair.at[0], sem)
    copy.start()
    copy.wait()


def pair_kernel(half, other, pair):
    pair[1] = other[...]


def halo_part(source, at, upper, acc, v1, wn, cat):
    cols, c1 = source.shape[2:]
    rows = acc.shape[1] - 3
    size = 2 * cols
    for f in range(2):
        for r in range(2):
            put_cat(cat, (f, r), silu(source[at[f], r].astype(F32)))

    def outer(k, _):
        i = jnp.where(upper, 0, 2)
        both = cat[...].reshape(2 * size, 3 * c1)
        part = dot(both[:size], v1[i])
        total = dot(both, wn[i].reshape(3 * c1, c1))
        m = jnp.where(upper, 0, rows)
        for f in range(2):
            acc[f, pl.ds(m, 2)] += (total[f * size : (f + 1) * size] + part).reshape(2, cols, c1)
        return 0

    def middle(k, _):
        r = jnp.where(upper, 1, 0)
        one = [cat[f, r] for f in range(2)]
        part = dot(one[0], v1[1])
        total = dot(jnp.concatenate(one, axis=0), wn[1].reshape(3 * c1, c1))
        m = jnp.where(upper, 0, rows + 1)
        for f in range(2):
            acc[f, m] += total[f * cols : (f + 1) * cols] + part
        return 0

    lax.fori_loop(0, 1, outer, 0)
    lax.fori_loop(0, 1, middle, 0)


def early_kernel(pair, w1, w2, w3, acc, v1, wn, v2, v3, cat, raw, sems):
    rows, cols, c1 = pair.shape[1:]
    second = lax.axis_index("sect") > 0

    def copy(t, i):
        target = raw.at[i, t] if t < 2 else wn.at[i]
        return pltpu.make_async_copy(w1.at[t, i], target, sems.at[i, t])

    for i in range(3):
        for t in range(3):
            copy(t, i).start()
    for r in range(rows):
        mine, other = pair[0, r].astype(F32), pair[1, r].astype(F32)
        put_cat(cat, (0, r), silu(jnp.where(second, other, mine)))
        put_cat(cat, (1, r), silu(mine))
    merge_space(w3, v3, 16)
    merge_space(w2, v2, 16)
    size = rows * cols
    acc[...] = jnp.zeros(acc.shape, F32)

    def tap(i, _):
        for t in range(2):
            copy(t, i).wait()
        merge_time(raw.at[i], v1.at[i])
        both = cat[...].reshape(2 * size, 3 * c1)
        part = dot(both[:size], v1[i])
        copy(2, i).wait()
        total = dot(both, wn[i].reshape(3 * c1, c1))
        for f in range(2):
            value = (total[f * size : (f + 1) * size] + part).reshape(rows, cols, c1)
            acc[f, pl.ds(2 - i, rows)] += value
        return 0

    lax.fori_loop(0, 3, tap, 0)


def middle_kernel(far, before, v1, wn, acc, cat):
    second = lax.axis_index("sect") > 0
    halo_part(far, (jnp.where(second, 0, 1), 1), jnp.logical_not(second), acc, v1, wn, cat)


def late_kernel(
    pair, far, near, before, v1, wn, b1, v2, b2, v3, b3, out, acc, hcat, mcat, lcat, wide, narrow, sems
):
    rows, cols, c1 = pair.shape[1:]
    c2 = b2.shape[0]
    c3 = b3.shape[0]
    second = lax.axis_index("sect") > 0
    tile = lax.axis_index("tile")
    first_tile = tile == 0
    last_tile = tile == lax.axis_size("tile") - 1

    def feature(f, r):
        if 2 <= r < rows + 2:
            mine = pair[0, r - 2].astype(F32)
            if f == 1:
                return mine
            return jnp.where(second, pair[1, r - 2].astype(F32), mine)
        above = r < 2
        r = r if above else r - rows - 2
        if above:
            own, other = (near[1 - f, r], far[1, r])
        else:
            own, other = (far[f, r], near[0, r])
        return jnp.where(second, own.astype(F32), other.astype(F32))

    mrows = rows + 2
    halo_part(near, (jnp.where(second, 1, 0), 0), second, acc, v1, wn, hcat)
    bias = b1[...].astype(F32)[None, :]
    for f in range(2):
        for m in range(mrows):
            v = acc[f, m] + bias + feature(f, m + 1)
            v = silu(v.astype(BF16).astype(F32))
            if m == 0:
                v = jnp.where(first_tile, 0.0, v)
            if m == mrows - 1:
                v = jnp.where(last_tile, 0.0, v)
            put_cat(mcat, (f, m), v)

    wins = mrows - 1
    bias = b2[...].astype(F32)[None, :]
    for b in range(2):
        lanes = slice(c1, 3 * c1) if b == 0 else slice(0, 2 * c1)
        early = jnp.zeros((wins * cols, 2 * c2), F32)
        now = [early, early]
        for i in range(2):
            lhs = [mcat[f, i : i + wins, :, lanes].reshape(wins * cols, 2 * c1) for f in range(2)]
            early = early + dot(lhs[0], v2[b, 0, i])
            for f in range(2):
                now[f] = now[f] + dot(lhs[f], v2[b, 1, i])
        for f in range(2):
            total = early + now[f]
            for w in range(wins):
                for a in range(2):
                    v = total[w * cols : (w + 1) * cols, a * c2 : (a + 1) * c2] + bias
                    v = silu(v)
                    if w == 0 and a == 0:
                        v = jnp.where(first_tile, 0.0, v)
                    if w == wins - 1 and a == 1:
                        v = jnp.where(last_tile, 0.0, v)
                    before, after = shifted(v)
                    r = 2 * w + a
                    if b == 0:
                        lcat[f, r, :, 0:c2] = before.astype(BF16)
                        lcat[f, r, :, 2 * c2 : 3 * c2] = v.astype(BF16)
                    else:
                        lcat[f, r, :, c2 : 2 * c2] = v.astype(BF16)
                        lcat[f, r, :, 3 * c2 : 4 * c2] = after.astype(BF16)

    lrows = 2 * wins
    wins = lrows - 1
    bias = b3[...].astype(F32)[None, :]
    for q in range(4):
        b = 1 if q % 2 == 0 else 0
        at = (0, c2, c2, 2 * c2)[q]
        lhs = jnp.concatenate(
            [lcat[f, i : i + wins, :, at : at + 2 * c2].reshape(wins * cols, 2 * c2) for f in range(2) for i in range(2)],
            axis=1,
        )
        total = dot(lhs, v3[b].reshape(8 * c2, 2 * c3))
        for o in range(4 * rows):
            a = 1 - o % 2
            w = (o + 1) // 2
            v = total[w * cols : (w + 1) * cols, a * c3 : (a + 1) * c3] + bias
            wide[o, pl.ds(q, cols, stride=4), :] = v
    copies = [pltpu.make_async_copy(narrow.at[o], out.at[o], sems.at[o]) for o in range(4 * rows)]
    for o in range(4 * rows):
        narrow[o] = wide[o].astype(BF16)
        copies[o].start()
    for copy in copies:
        copy.wait()


def in_vmem(x):
    return pltpu.with_memory_space_constraint(x, pltpu.VMEM)


def per_device(features, conv_first, bias_first, conv_second, bias_second, conv_third, bias_third):
    own = features[0]
    rows, cols, c1 = own.shape
    c2 = conv_second.shape[4]
    c3 = conv_third.shape[4]
    tiles = lax.axis_size("tile")
    swap = [(0, 1), (1, 0)]
    apart = [(i + 1, tiles + i) for i in range(tiles - 1)]
    apart += [(tiles + i, i + 1) for i in range(tiles - 1)]
    vmem = pl.BlockSpec(memory_space=pltpu.VMEM)
    anywhere = pl.BlockSpec(memory_space=pl.ANY)

    other = lax.ppermute(own, "sect", swap)
    pair_shape = pltpu.VMEM((2, rows, cols, c1), BF16)
    half = pl.pallas_call(
        load_kernel,
        out_shape=pair_shape,
        in_specs=[anywhere],
        out_specs=vmem,
        scratch_shapes=[pltpu.SemaphoreType.DMA],
        cost_estimate=pl.CostEstimate(flops=6_000_000_000, bytes_accessed=1024, transcendentals=0),
        compiler_params=pltpu.CompilerParams(vmem_limit_bytes=1 << 20),
    )(pltpu.with_memory_space_constraint(own, pltpu.HBM))
    pair = pl.pallas_call(
        pair_kernel,
        out_shape=pair_shape,
        in_specs=[vmem] * 2,
        out_specs=vmem,
        input_output_aliases={0: 0},
        cost_estimate=pl.CostEstimate(flops=6_000_000_000, bytes_accessed=1024, transcendentals=0),
        compiler_params=pltpu.CompilerParams(vmem_limit_bytes=1 << 20),
    )(in_vmem(half), in_vmem(other))
    if rows == 2:
        edge = pair
    else:
        edge = jnp.where(lax.axis_index("sect") == 1, pair[:, rows - 2 :], pair[:, :2])
    far = lax.ppermute(edge, ("sect", "tile"), apart)
    near = lax.ppermute(far, "sect", swap)
    acc, v1, wn, v2, v3 = pl.pallas_call(
        early_kernel,
        out_shape=[
            pltpu.VMEM((2, rows + 3, cols, c1), F32),
            pltpu.VMEM((3, 3 * c1, c1), BF16),
            pltpu.VMEM((3, 3, c1, c1), BF16),
            pltpu.VMEM((2, 2, 2, 2 * c1, 2 * c2), BF16),
            pltpu.VMEM((2, 2, 2, 2 * c2, 2 * c3), BF16),
        ],
        in_specs=[vmem, anywhere, vmem, vmem],
        out_specs=[vmem] * 5,
        scratch_shapes=[
            pltpu.VMEM((2, rows, cols, 3 * c1), BF16),
            pltpu.VMEM((3, 2, 3, c1, c1), BF16),
            pltpu.SemaphoreType.DMA((3, 3)),
        ],
        cost_estimate=pl.CostEstimate(flops=6_000_000_000, bytes_accessed=1024, transcendentals=0),
        compiler_params=pltpu.CompilerParams(vmem_limit_bytes=16 << 20),
    )(
        in_vmem(pair),
        pltpu.with_memory_space_constraint(conv_first, pltpu.HBM),
        in_vmem(conv_second),
        in_vmem(conv_third),
    )
    acc_shape = pltpu.VMEM((2, rows + 3, cols, c1), F32)
    acc = pl.pallas_call(
        middle_kernel,
        out_shape=acc_shape,
        in_specs=[vmem] * 4,
        out_specs=vmem,
        input_output_aliases={1: 0},
        scratch_shapes=[pltpu.VMEM((2, 2, cols, 3 * c1), BF16)],
        cost_estimate=pl.CostEstimate(flops=2_000_000_000, bytes_accessed=1024, transcendentals=0),
        compiler_params=pltpu.CompilerParams(vmem_limit_bytes=8 << 20),
    )(in_vmem(far), in_vmem(acc), in_vmem(v1), in_vmem(wn))
    out, _ = pl.pallas_call(
        late_kernel,
        out_shape=[jax.ShapeDtypeStruct((4 * rows, 4 * cols, c3), BF16), acc_shape],
        in_specs=[vmem] * 11,
        out_specs=[anywhere, vmem],
        input_output_aliases={3: 1},
        scratch_shapes=[
            pltpu.VMEM((2, 2, cols, 3 * c1), BF16),
            pltpu.VMEM((2, rows + 2, cols, 3 * c1), BF16),
            pltpu.VMEM((2, 2 * rows + 2, cols, 4 * c2), BF16),
            pltpu.VMEM((4 * rows, 4 * cols, c3), F32),
            pltpu.VMEM((4 * rows, 4 * cols, c3), BF16),
            pltpu.SemaphoreType.DMA((4 * rows,)),
        ],
        cost_estimate=pl.CostEstimate(flops=8_000_000_000, bytes_accessed=1024, transcendentals=0),
        compiler_params=pltpu.CompilerParams(vmem_limit_bytes=14 << 20),
    )(
        in_vmem(pair),
        in_vmem(far),
        in_vmem(near),
        in_vmem(acc),
        in_vmem(v1),
        in_vmem(wn),
        bias_first,
        in_vmem(v2),
        bias_second,
        in_vmem(v3),
        bias_third,
    )
    return out[None]


def solution(mesh):
    return jax.shard_map(
        per_device,
        mesh=mesh,
        in_specs=(P(("groups", "sect"), "tile", None, None), P(), P(), P(), P(), P(), P()),
        out_specs=P(("groups", "sect"), "tile", None, None),
        check_vma=False,
    )
```
